128 devices in a mesh: dp: 16 (over z_lo, x, core), ctx: 8 (over y, z_hi).
Axes of the slice: x: 4, y: 4, z: 4 (z_hi: 2, z_lo: 2; z = z_hi * 2 + z_lo), core: 2. Of those that a mesh axis runs over, the one named last changes fastest.
Arguments:
- inputs: bfloat16 [16, 2048, 4096], P('dp', 'ctx'), may hold values from -0.4375 to 0.4375
- queries: bfloat16 [16, 2048, 512], P('dp', 'ctx'), may hold values from -6 to 6
- keys: bfloat16 [16, 2048, 512], P('dp', 'ctx'), may hold values from -6 to 6
- values: bfloat16 [16, 2048, 512], P('dp', 'ctx'), may hold values from -6 to 6
- attn_out: bfloat16 [16, 2048, 512], P('dp', 'ctx'), may hold values from -6 to 6
- grad_out: bfloat16 [16, 2048, 512], P('dp', 'ctx'), may hold values from -96 to 96
- lse_shift: float32 [16, 4, 2048], P('dp', None, 'ctx'), may hold values from -1 to 1
- labels: int32 [16, 16], P('dp'), may hold values from 0 to 2, as said below
- layout: int32 [16, 16], P('dp'), may hold values from 0 to 15, each once within a row
Outputs:
- grad_q: bfloat16 [16, 2048, 512], P('dp', 'ctx')
- grad_k: bfloat16 [16, 2048, 512], P('dp', 'ctx')
- grad_v: bfloat16 [16, 2048, 512], P('dp', 'ctx')
- grad_w: float32 [4096, 1536], P(('dp', 'ctx'))
The draws below stay inside these ranges and needn't reach their ends.
Inputs may be any that keep to these rules, and one draw needn't show every extreme that they name: `labels`: in a pair's natural tile order the prompt (label 0) comes first and covers 8 to 12 tiles, then the chosen response (label 1), then the rejected response (label 2), each response one tile or more. `layout`: each pair's row names every tile once.
All inputs are finite; a program needn't handle non-finite values.
Results may differ from the reference program's by a relative error of at most 0.0058.
Values may be sent and summed in bfloat16 or wider, within the bound.
A program may use at most 128 MiB of HBM per device.

```python
import math
import jax
import jax.numpy as jnp
from jax import lax

D = 4096
HEAD_DIM = 128
HEADS = 4
TILE = 128
TOK_DEV = 256
PAIRS = 16
LENGTH = 2048
NTILES = 16
N_CTX = 8


def draw_labels(key, part):

    def per_pair(pair_key):
        prompt_key, chosen_key = jax.random.split(pair_key)
        prompt = jax.random.randint(prompt_key, (), NTILES // 2, 3 * NTILES // 4 + 1)
        remain = NTILES - prompt
        chosen = jax.random.randint(chosen_key, (), 1, remain)
        tile_ids = jnp.arange(NTILES)
        return jnp.where(tile_ids < prompt, 0, jnp.where(tile_ids < prompt + chosen, 1, 2)).astype(jnp.int32)
    return jax.vmap(per_pair)(jax.random.split(jax.random.fold_in(key, 7), PAIRS))


def raised(values, key, source, target, blocks, factor):
    def block_of(dim):
        return (jnp.arange(values.shape[dim]) // (values.shape[dim] // blocks)).reshape((-1,) + (1,) * (values.ndim - 1 - dim))

    near = jax.random.permutation(key, blocks)[block_of(target)]
    far = (block_of(target) + blocks // 2) % blocks
    return jnp.where((block_of(source) == near) | (block_of(source) == far), factor * values, values)


def shard_levels(rng, extent, cuts, smallest, top_value):
    loudness, own = 1.0, jax.random.fold_in(rng, 6)
    for dim, parts in cuts:
        steps = jnp.exp(jax.random.uniform(jax.random.fold_in(own, dim), (parts,), jnp.float32, smallest / len(cuts), top_value / len(cuts)))
        loudness = loudness * jnp.repeat(steps, extent[dim] // parts).reshape([-1 if axis == dim else 1 for axis in range(len(extent))])
    return loudness


def noise(own_key, shape, width, bound, cuts=(), kind=jnp.bfloat16):
    gain = shard_levels(own_key, shape, cuts, -0.22, 0.18) if cuts else 1.0
    entries = jax.random.normal(own_key, shape, jnp.float32) * width * gain
    return jnp.minimum(jnp.maximum(entries, -bound), bound).astype(kind)


def bell_draw_with(stream_key, dims, width, reach, cuts, heavy, held_as=jnp.bfloat16):
    values = width * jax.random.normal(stream_key, dims, jnp.float32)
    if cuts:
        values = values * shard_levels(stream_key, dims, cuts, -0.22, 0.18)
    return jnp.clip(raised(values, jax.random.fold_in(stream_key, 3), *heavy), -reach, reach).astype(held_as)


def setup_inputs(seed: int = 0) -> dict:
    seeds = jax.random.split(jax.random.key(seed), 10)
    inputs = bell_draw_with(seeds[0], (PAIRS, LENGTH, D), 0.05, 0.4375, ((0, 16), (1, 8)), (1, 2, 8, 2.0))
    queries = noise(seeds[1], (PAIRS, LENGTH, HEADS * HEAD_DIM), 1.0, 6.0, ((0, 16), (1, 8)))
    keys = noise(seeds[2], (PAIRS, LENGTH, HEADS * HEAD_DIM), 1.0, 6.0, ((0, 16), (1, 8)))
    values = noise(seeds[3], (PAIRS, LENGTH, HEADS * HEAD_DIM), 1.0, 6.0, ((0, 16), (1, 8)))
    attn_out = noise(seeds[4], (PAIRS, LENGTH, HEADS * HEAD_DIM), 1.0, 6.0, ((0, 16), (1, 8)))
    grad_out = noise(seeds[5], (PAIRS, LENGTH, HEADS * HEAD_DIM), 16.0, 96.0, ((0, 16), (1, 8)))
    lse_shift = jnp.clip(jax.random.uniform(seeds[6], (PAIRS, HEADS, LENGTH), jnp.float32, -1.0, 1.0) * shard_levels(seeds[6], (PAIRS, HEADS, LENGTH), ((0, 16), (2, 8)), -0.4, 0.0), -1.0, 1.0)
    labels = draw_labels(jax.random.fold_in(seeds[9], 71), 0)
    layout = jax.vmap(lambda own: jax.random.permutation(own, NTILES))(jax.random.split(seeds[8], PAIRS)).reshape((PAIRS, NTILES)).astype(jnp.int32)
    return {"inputs": inputs, "queries": queries, "keys": keys, "values": values, "attn_out": attn_out, "grad_out": grad_out, "lse_shift": lse_shift, "labels": labels, "layout": layout}


def stored_labels(label_row, layout_row):
    tile_ids = jnp.arange(label_row.shape[0], dtype=jnp.int32)
    matches = (layout_row[:, None] == tile_ids[None, :]).astype(jnp.int32)
    return lax.optimization_barrier(jnp.sum(matches * label_row[None, :], axis=1)).astype(jnp.int32)

def log_norms(tile_labels, own_labels, shift_rows):
    label_kinds = jnp.arange(3, dtype=jnp.int32)
    per_kind = lax.optimization_barrier(jnp.sum((tile_labels[:, None] == label_kinds[None, :]).astype(jnp.int32), axis=0)).astype(jnp.int32) * TILE
    own_match = (own_labels[:, None] == label_kinds[None, :]).astype(jnp.int32)
    own_count = lax.optimization_barrier(jnp.sum(own_match * per_kind[None, :], axis=1)).astype(jnp.int32)
    visible = per_kind[0] + jnp.where(own_labels != 0, own_count, 0)
    return jnp.log(visible.astype(jnp.float32))[None, :] + shift_rows

def split_heads(matrix_rows):
    return matrix_rows.reshape(matrix_rows.shape[0], HEADS, HEAD_DIM).astype(jnp.float32)

def block_core(query_rows, grad_rows, log_norm, deltas, query_labels, key_rows, value_rows, key_labels):
    scaling = 1.0 / math.sqrt(HEAD_DIM)
    scores = jnp.einsum('qhd,khd->hqk', split_heads(query_rows), split_heads(key_rows)) * scaling
    allowed = (key_labels[None, :] == 0) | (query_labels[:, None] == key_labels[None, :])
    weights = jnp.where(allowed[None], jnp.exp(scores - log_norm[:, :, None]), 0.0)
    through = jnp.einsum('qhd,khd->hqk', split_heads(grad_rows), split_heads(value_rows))
    dscore = (weights * (through - deltas[:, :, None]) * scaling).astype(jnp.bfloat16)
    return (weights.astype(jnp.bfloat16), dscore)

def row_part(matrix, key_rows):
    result = jnp.einsum('hqk,khd->qhd', matrix.astype(jnp.float32), split_heads(key_rows))
    return result.reshape(matrix.shape[1], HEADS * HEAD_DIM)

def column_part(matrix, query_rows):
    result = jnp.einsum('hqk,qhd->khd', matrix.astype(jnp.float32), split_heads(query_rows))
    return result.reshape(matrix.shape[2], HEADS * HEAD_DIM)

def pair_grads(feature_rows, query_rows, key_rows, value_rows, attn_rows, grad_rows, shift_rows, label_row, layout_row):
    tile_labels = stored_labels(label_row, layout_row)
    token_labels = jnp.repeat(tile_labels, TILE, total_repeat_length=LENGTH)
    log_norm = log_norms(tile_labels, token_labels, shift_rows)
    deltas = jnp.einsum('thd,thd->ht', split_heads(grad_rows), split_heads(attn_rows))

    def visit(totals, block_index):
        first_row = block_index * TOK_DEV
        query_block = lax.dynamic_slice_in_dim(query_rows, first_row, TOK_DEV, 0)
        grad_block = lax.dynamic_slice_in_dim(grad_rows, first_row, TOK_DEV, 0)
        norm_block = lax.dynamic_slice_in_dim(log_norm, first_row, TOK_DEV, 1)
        delta_block = lax.dynamic_slice_in_dim(deltas, first_row, TOK_DEV, 1)
        label_block = lax.dynamic_slice_in_dim(token_labels, first_row, TOK_DEV, 0)
        weights, dscore = block_core(query_block, grad_block, norm_block, delta_block, label_block, key_rows, value_rows, token_labels)
        sum_k = totals[0] + column_part(dscore, query_block)
        sum_v = totals[1] + column_part(weights, grad_block)
        return ((sum_k, sum_v), row_part(dscore, key_rows).astype(jnp.bfloat16))
    zero_rows = jnp.zeros((LENGTH, HEADS * HEAD_DIM), jnp.float32)
    (sum_k, sum_v), grad_q = lax.scan(visit, (zero_rows, zero_rows), jnp.arange(N_CTX, dtype=jnp.int32))
    grad_q = grad_q.reshape(LENGTH, HEADS * HEAD_DIM)
    grad_k = sum_k.astype(jnp.bfloat16)
    grad_v = sum_v.astype(jnp.bfloat16)
    stacked = jnp.concatenate([grad_q, grad_k, grad_v], axis=1)
    weight_term = jnp.dot(feature_rows.T, stacked, preferred_element_type=jnp.float32)
    return (grad_q, grad_k, grad_v, weight_term)

def reference(inputs, queries, keys, values, attn_out, grad_out, lse_shift, labels, layout):

    def per_pair(total_w, pair_items):
        grad_q, grad_k, grad_v, weight_term = pair_grads(*pair_items)
        return (total_w + weight_term, (grad_q, grad_k, grad_v))
    start_w = jnp.zeros((D, 3 * HEADS * HEAD_DIM), jnp.float32)
    grad_w, (grad_q, grad_k, grad_v) = lax.scan(per_pair, start_w, (inputs, queries, keys, values, attn_out, grad_out, lse_shift, labels, layout))
    return (grad_q, grad_k, grad_v, grad_w)
```

```python
import functools
import math

import jax
import jax.numpy as jnp
from jax import lax
from jax.experimental import pallas as pl
from jax.experimental.pallas import tpu as pltpu
from jax.sharding import PartitionSpec as P

HEADS = 4
HD = 128
TOK = 256
LOG2E = math.log2(math.e)
SCALE = 1.0 / math.sqrt(HD)
HIDDEN = 1e30
MESH = pl.DeviceIdType.MESH
F32 = jnp.float32
BF16 = jnp.bfloat16
ANY = pl.BlockSpec(memory_space=pl.ANY)
VM = pl.BlockSpec(memory_space=pltpu.VMEM)
SM = pl.BlockSpec(memory_space=pltpu.SMEM)


def place():
    dp = lax.axis_index("dp")
    ctx = lax.axis_index("ctx")
    core = lax.rem(dp, 2)
    x = lax.rem(dp // 2, 4)
    z_lo = dp // 8
    y = ctx // 2
    z_hi = lax.rem(ctx, 2)
    return core, x, y, z_lo, z_hi, dp, ctx


def greet(devices):
    barrier = pltpu.get_barrier_semaphore()
    for d in devices:
        pl.semaphore_signal(barrier, inc=1, device_id=d, device_id_type=MESH)
    return lambda: pl.semaphore_wait(barrier, len(devices))


def remote(src, dst, send, recv, device):
    return pltpu.make_async_remote_copy(
        src_ref=src, dst_ref=dst, send_sem=send, recv_sem=recv,
        device_id=device, device_id_type=MESH,
    )


def tile_rows(labels, layout, ctx):
    n0 = jnp.int32(0)
    n1 = jnp.int32(0)
    for j in range(16):
        lab = labels[0, j]
        n0 = n0 + jnp.where(lab == 0, 1, 0)
        n1 = n1 + jnp.where(lab == 1, 1, 0)
    n2 = 16 - n0 - n1
    out = []
    for t in range(2):
        lab = labels[0, layout[0, 2 * ctx + t]]
        own = jnp.where(lab == 1, n1, jnp.where(lab == 2, n2, 0))
        count = ((n0 + own) * 128).astype(F32)
        out.append((lab, jnp.log(jnp.full((1, 128), count, F32))))
    return out


def spread_kernel(
    labels, layout, lse, do_v, o_v, q, k, v, do, x_in,
    qo, doo, ko, vo, auxo, xo,
    aux, send, recv, fsend, frecv, xsend, xrecv,
):
    core, x, y, z_lo, z_hi, dp, ctx = place()
    base = dp - core
    targets = [(base + 1 - z_hi, h * 2 + core) for h in range(4)]
    sources = [(base + z_hi, s * 2 + 1 - core) for s in range(4)]
    sibling = (base + 1 - core, ctx)
    ready = greet(targets + sources + [sibling])

    tiles = tile_rows(labels, layout, ctx)
    labs = jnp.concatenate(
        [jnp.full((1, 128), lab, jnp.int32) for lab, _ in tiles], axis=1
    )
    logs = jnp.concatenate([lg for _, lg in tiles], axis=1)
    for h in range(HEADS):
        cols = slice(h * HD, (h + 1) * HD)
        prod = do_v[0, :, cols].astype(F32) * o_v[0, :, cols].astype(F32)
        delta = jnp.sum(prod.T, axis=0, keepdims=True)
        ln = (logs + lse[0, h : h + 1, :]) * LOG2E
        aux[h, 0:1, :] = ln
        aux[h, 1:2, :] = jnp.where(labs == 1, ln, HIDDEN)
        aux[h, 2:3, :] = jnp.where(labs == 2, ln, HIDDEN)
        aux[h, 3:4, :] = delta
        aux[h, 4:5, :] = labs.astype(F32)
        aux[h, 5:8, :] = jnp.zeros((3, TOK), F32)

    ready()
    xs = []
    for i in range(8):
        c = remote(
            x_in.at[0, :, pl.ds(pl.multiple_of((2 * i + 1 - core) * 256, 256), 256)],
            xo.at[i], xsend.at[i], xrecv.at[i], sibling,
        )
        c.start()
        xs.append(c)
    copies = []
    arrays = ((q, qo), (do, doo), (None, auxo), (k, ko), (v, vo))
    for n, (src, dst) in enumerate(arrays):
        for h in range(HEADS):
            if src is None:
                s = aux.at[h]
            else:
                s = src.at[0, :, h * HD : (h + 1) * HD]
            c = remote(s, dst.at[y], send.at[n, h], recv.at[n, y], targets[h])
            c.start()
            copies.append(c)

    def arrived(n, s):
        dst = arrays[n][1].at[s]
        remote(dst, dst, send.at[n, s], recv.at[n, s], sibling).wait_recv()

    fwd = []
    for s in range(4):
        for n in range(3):
            arrived(n, s)
            dst = arrays[n][1]
            c = remote(dst.at[s], dst.at[4 + s], fsend.at[n, s], frecv.at[n, s], sibling)
            c.start()
            fwd.append(c)
    for s in range(4):
        arrived(3, s)
        arrived(4, s)
    for c in copies:
        c.wait_send()
    for c in fwd:
        c.wait()
    for c in xs:
        c.wait()


def spread(labels, layout, lse, q, k, v, o, do, x_in):
    blk = lambda n: jax.ShapeDtypeStruct((n, TOK, HD), BF16)
    return pl.pallas_call(
        spread_kernel,
        out_shape=(
            blk(8), blk(8), blk(4), blk(4),
            jax.ShapeDtypeStruct((8, 8, TOK), F32),
            jax.ShapeDtypeStruct((8, TOK, 256), BF16),
        ),
        in_specs=[SM, SM, VM, VM, VM, ANY, ANY, ANY, ANY, ANY],
        out_specs=(ANY,) * 6,
        scratch_shapes=[
            pltpu.VMEM((4, 8, TOK), F32),
            pltpu.SemaphoreType.DMA((5, 4)),
            pltpu.SemaphoreType.DMA((5, 4)),
            pltpu.SemaphoreType.DMA((3, 4)),
            pltpu.SemaphoreType.DMA((3, 4)),
            pltpu.SemaphoreType.DMA((8,)),
            pltpu.SemaphoreType.DMA((8,)),
        ],
        compiler_params=pltpu.CompilerParams(collective_id=0, has_side_effects=True),
        name="spread",
    )(labels, layout, lse, do, o, q, k, v, do, x_in)


def dot_t(a, b):
    return lax.dot_general(a, b, (((1,), (1,)), ((), ())), preferred_element_type=F32)


def dot_n(a, b):
    return lax.dot_general(a, b, (((1,), (0,)), ((), ())), preferred_element_type=F32)


def dot_l(a, b):
    return lax.dot_general(a, b, (((0,), (0,)), ((), ())), preferred_element_type=F32)


def attention_kernel(q, do, k, v, aux, dk, dv, dq_out, dk_acc, dv_acc, p_s, ds_s):
    dk_acc[...] = jnp.zeros_like(dk_acc)
    dv_acc[...] = jnp.zeros_like(dv_acc)
    k_all = k[...].reshape(4 * TOK, HD)
    v_all = v[...].reshape(4 * TOK, HD)

    def step(c, carry):
        qc = q[c]
        doc = do[c]
        s = dot_t(k_all, qc)
        d = dot_t(v_all, doc)
        rows = aux[c]
        delta = rows[3:4, :]
        for t in range(8):
            part = slice(t * 128, (t + 1) * 128)
            lab = aux[t // 2, 4:5, (t % 2) * 128 : (t % 2) * 128 + 1]
            row = jnp.where(
                lab == 0.0, rows[0:1, :], jnp.where(lab == 1.0, rows[1:2, :], rows[2:3, :])
            )
            p = jnp.exp2(s[part] * (SCALE * LOG2E) - row)
            p_s[part, :] = p.astype(BF16)
            ds_s[part, :] = (p * (d[part] - delta) * SCALE).astype(BF16)
        p_b = p_s[...]
        ds_b = ds_s[...]
        dv_acc[...] += dot_n(p_b, doc)
        dk_acc[...] += dot_n(ds_b, qc)
        dq = dot_l(ds_b, k_all)
        dq_out[c] = dq.astype(BF16)
        return carry

    lax.fori_loop(0, 8, step, 0)
    dk[...] = dk_acc[...].astype(BF16).reshape(4, TOK, HD)
    dv[...] = dv_acc[...].astype(BF16).reshape(4, TOK, HD)


def attention(q, do, k, v, aux):
    blk = lambda n: jax.ShapeDtypeStruct((n, TOK, HD), BF16)

    return pl.pallas_call(
        attention_kernel,
        out_shape=(blk(4), blk(4), blk(8)),
        in_specs=[VM] * 5,
        out_specs=(VM,) * 3,
        scratch_shapes=[
            pltpu.VMEM((1024, HD), F32),
            pltpu.VMEM((1024, HD), F32),
            pltpu.VMEM((1024, TOK), BF16),
            pltpu.VMEM((1024, TOK), BF16),
        ],
        name="attention",
    )(q, do, k, v, aux)


def collect_kernel(
    dk, dv, dq, dq_v, g,
    other, total, osend, orecv, send, recv, fsend, frecv,
):
    core, x, y, z_lo, z_hi, dp, ctx = place()
    base = dp - core
    targets = [(base + 1 - z_hi, h * 2 + core) for h in range(4)]
    owners = [(base + z_hi, s * 2 + 1 - core) for s in range(4)]
    sibling = (base + 1 - core, ctx)
    greet(targets + owners + [sibling])()

    swap = remote(dq.at[pl.ds(4, 4)], other, osend, orecv, sibling)
    swap.start()
    copies = []

    def give(t, s, src):
        c = remote(src, g.at[0, t, y], send.at[t, s], recv.at[t, y], owners[s])
        c.start()
        copies.append(c)

    for s in range(4):
        give(1, s, dk.at[s])
    for s in range(4):
        give(2, s, dv.at[s])
    swap.wait()
    for s in range(4):
        total[s] = (dq_v[s].astype(F32) + other[s].astype(F32)).astype(BF16)
    for s in range(4):
        give(0, s, total.at[s])
    fwd = []
    for t in (1, 2, 0):
        for h in range(4):
            piece = g.at[0, t, h]
            remote(piece, piece, send.at[t, h], recv.at[t, h], sibling).wait_recv()
            c = remote(piece, g.at[1, t, h], fsend.at[t, h], frecv.at[t, h], sibling)
            c.start()
            fwd.append(c)
    for c in copies:
        c.wait_send()
    for c in fwd:
        c.wait()


def collect(dk, dv, dq):
    return pl.pallas_call(
        collect_kernel,
        out_shape=jax.ShapeDtypeStruct((2, 3, 4, TOK, HD), BF16),
        in_specs=[ANY, ANY, ANY, VM],
        out_specs=ANY,
        scratch_shapes=[
            pltpu.VMEM((4, TOK, HD), BF16),
            pltpu.VMEM((4, TOK, HD), BF16),
            pltpu.SemaphoreType.DMA,
            pltpu.SemaphoreType.DMA,
            pltpu.SemaphoreType.DMA((3, 4)),
            pltpu.SemaphoreType.DMA((3, 4)),
            pltpu.SemaphoreType.DMA((3, 4)),
            pltpu.SemaphoreType.DMA((3, 4)),
        ],
        compiler_params=pltpu.CompilerParams(collective_id=1, has_side_effects=True),
        name="collect",
    )(dk, dv, dq, dq)


def project_kernel(core, xa, xb, g, part, gq, gk, gv, rhs):
    i = pl.program_id(0)

    @pl.when(i == 0)
    def _():
        for t, out in enumerate((gq, gk, gv)):
            for h in range(4):
                for c in range(2):
                    rhs[c * TOK : (c + 1) * TOK, (t * 4 + h) * HD : (t * 4 + h + 1) * HD] = g[c, t, h]
                out[0, :, h * HD : (h + 1) * HD] = g[0, t, h]

    lhs = jnp.concatenate([xa[0].T, xb[0].T], axis=1)
    for n in range(6):
        res = dot_n(lhs, rhs[:, n * 256 : (n + 1) * 256])
        part[n, 0] = res.astype(BF16).reshape(8, 32, 256)


def project(core, x_in, xo, g):
    grad = jax.ShapeDtypeStruct((1, TOK, HEADS * HD), BF16)
    gspec = pl.BlockSpec((1, TOK, HEADS * HD), lambda i, c: (0, 0, 0))
    return pl.pallas_call(
        project_kernel,
        out_shape=(jax.ShapeDtypeStruct((6, 8, 8, 32, 256), BF16), grad, grad, grad),
        grid_spec=pltpu.PrefetchScalarGridSpec(
            num_scalar_prefetch=1,
            grid=(8,),
            in_specs=[
                pl.BlockSpec((1, TOK, 256), lambda i, c: (0, 0, 2 * i + c[0])),
                pl.BlockSpec((1, TOK, 256), lambda i, c: (i, 0, 0)),
                pl.BlockSpec((2, 3, 4, TOK, HD), lambda i, c: (0, 0, 0, 0, 0)),
            ],
            out_specs=(
                pl.BlockSpec((6, 1, 8, 32, 256), lambda i, c: (0, i, 0, 0, 0)),
                gspec, gspec, gspec,
            ),
            scratch_shapes=[pltpu.VMEM((2 * TOK, 1536), BF16)],
        ),
        name="project",
    )(core, x_in, xo, g)


ORDERS = ("xyz", "yzx", "zxy")
SIZES = {"l": 2, "x": 4, "y": 4, "h": 2}


def reduce_kernel(part, out, *scratch):
    core, x, y, z_lo, z_hi, dp, ctx = place()
    z = z_hi * 2 + z_lo
    here = {"x": x, "y": y, "z": z}

    def device(axis, by):
        c = dict(here)
        c[axis] = lax.rem(c[axis] + by + 4, 4)
        return (lax.rem(c["z"], 2) * 8 + c["x"] * 2 + core, c["y"] * 2 + c["z"] // 2)

    neighbours = [device(a, by) for a in "xyz" for by in (1, -1)]
    ready = greet(neighbours)
    bufs = scratch[:27]
    send, recv = scratch[27:]
    ready()

    def pick(ref, dims, axis, coord):
        if axis == "z":
            want = {"l": lax.rem(coord, 2), "h": coord // 2}
        else:
            want = {axis: coord}
        idx = tuple(want[d] if d in want else slice(None) for d in dims)
        return idx, "".join(d for d in dims if d not in want)

    state = []
    for n in range(3):
        state.append(((lambda half, n=n: part.at[2 * n + half]), "lxyh"))

    for stage in range(3):
        jobs = []
        for n in range(3):
            axis = ORDERS[n][stage]
            got, comb, tot = bufs[(stage * 3 + n) * 3 : (stage * 3 + n) * 3 + 3]
            view, dims = state[n]
            a = here[axis]
            right = lax.rem(a + 1, 4)
            left = lax.rem(a + 3, 4)
            opp = lax.rem(a + 2, 4)
            dev_r, dev_l = device(axis, 1), device(axis, -1)
            ss, rs = send.at[stage, n], recv.at[stage, n]

            def piece(half, coord, view=view, dims=dims, axis=axis):
                idx, _ = pick(None, dims, axis, coord)
                return view(half).at[idx]

            rest = pick(None, dims, axis, 0)[1]

            def job(msg, src, dev, got=got, ss=ss, rs=rs):
                return remote(src, got.at[msg], ss.at[msg], rs.at[msg], dev)

            first = [
                job(0, piece(0, opp), dev_r),
                job(1, piece(1, opp), dev_l),
                job(2, piece(1, right), dev_r),
                job(3, piece(0, left), dev_l),
            ]
            jobs.append((n, piece, first, job, got, comb, tot, rest, a, right, left, dev_r, dev_l))
        for m in range(4):
            for j in jobs:
                j[2][m].start()
        second = []
        for msg in (0, 1):
            for n, piece, first, job, got, comb, tot, rest, a, right, left, dev_r, dev_l in jobs:
                first[msg].wait_recv()
                mine = piece(msg, right if msg == 0 else left)
                comb[msg] = (got[msg].astype(F32) + mine[...].astype(F32)).astype(BF16)
                c = job(4 + msg, comb.at[msg], dev_r if msg == 0 else dev_l)
                c.start()
                second.append(c)
        for n, piece, first, job, got, comb, tot, rest, a, right, left, dev_r, dev_l in jobs:
            first[3].wait_recv()
            second[n].wait_recv()
            first[2].wait_recv()
            second[3 + n].wait_recv()
            for half, raw, summed in ((0, 3, 4), (1, 2, 5)):
                total = (
                    piece(half, a)[...].astype(F32)
                    + got[raw].astype(F32)
                    + got[summed].astype(F32)
                )
                if stage < 2:
                    tot[half] = total.astype(BF16)
                else:
                    out[:, n * 512 + half * 256 : n * 512 + half * 256 + 256] = total
            state[n] = ((lambda half, tot=tot: tot.at[half]), rest)
        for j in jobs:
            for c in j[2]:
                c.wait_send()
        for c in second:
            c.wait_send()


def reduce(part):
    part = part.reshape(6, 2, 4, 4, 2, 32, 256)
    scratch = []
    dims = ["lxyh"] * 3
    for stage in range(3):
        for n in range(3):
            axis = ORDERS[n][stage]
            drop = "lh" if axis == "z" else axis
            rest = "".join(d for d in dims[n] if d not in drop)
            dims[n] = rest
            shape = tuple(SIZES[d] for d in rest) + (32, 256)
            scratch.append(pltpu.VMEM((6,) + shape, BF16))
            scratch.append(pltpu.VMEM((2,) + shape, BF16))
            scratch.append(pltpu.VMEM((2,) + shape, BF16))
    scratch += [pltpu.SemaphoreType.DMA((3, 3, 6)), pltpu.SemaphoreType.DMA((3, 3, 6))]
    return pl.pallas_call(
        reduce_kernel,
        out_shape=jax.ShapeDtypeStruct((32, 1536), F32),
        in_specs=[VM],
        out_specs=VM,
        scratch_shapes=scratch,
        compiler_params=pltpu.CompilerParams(collective_id=2, has_side_effects=True),
        name="reduce",
    )(part)


def per_device(inputs, queries, keys, values, attn_out, grad_out, lse_shift, labels, layout):
    q, do, k, v, aux, xo = spread(
        labels, layout, lse_shift, queries, keys, values, attn_out, grad_out, inputs
    )
    dk, dv, dq = attention(q, do, k, v, aux)
    g = collect(dk, dv, dq)
    core = lax.rem(lax.axis_index("dp"), 2).astype(jnp.int32).reshape(1)
    part, gq, gk, gv = project(core, inputs, xo, g)
    gw = reduce(part)
    return gq, gk, gv, gw


def solution(mesh):
    tok = P("dp", "ctx", None)
    return jax.shard_map(
        per_device,
        mesh=mesh,
        in_specs=(tok,) * 6 + (P("dp", None, "ctx"), P("dp", None), P("dp", None)),
        out_specs=(tok, tok, tok, P(("dp", "ctx"), None)),
        check_vma=False,
    )
```

```python
import functools
import math

import jax
import jax.numpy as jnp
from jax import lax
from jax.experimental import pallas as pl
from jax.experimental.pallas import tpu as pltpu
from jax.sharding import PartitionSpec as P

HEADS = 4
HD = 128
TOK = 256
LOG2E = math.log2(math.e)
SCALE = 1.0 / math.sqrt(HD)
HIDDEN = 1e30
MESH = pl.DeviceIdType.MESH
F32 = jnp.float32
BF16 = jnp.bfloat16
ANY = pl.BlockSpec(memory_space=pl.ANY)
VM = pl.BlockSpec(memory_space=pltpu.VMEM)
SM = pl.BlockSpec(memory_space=pltpu.SMEM)


def place():
    dp = lax.axis_index("dp")
    ctx = lax.axis_index("ctx")
    core = lax.rem(dp, 2)
    x = lax.rem(dp // 2, 4)
    z_lo = dp // 8
    y = ctx // 2
    z_hi = lax.rem(ctx, 2)
    return core, x, y, z_lo, z_hi, dp, ctx


def flip(a, b):
    return lax.rem(a + b, 2)


def target(h):
    core, x, y, z_lo, z_hi, dp, ctx = place()
    return (dp - core + flip(1 + z_hi, y), h * 2 + flip(core, h))


def owner(s):
    core, x, y, z_lo, z_hi, dp, ctx = place()
    return (dp - core + flip(z_hi, y), s * 2 + flip(1 + core, s))


def greet(devices):
    barrier = pltpu.get_barrier_semaphore()
    for d in devices:
        pl.semaphore_signal(barrier, inc=1, device_id=d, device_id_type=MESH)
    return lambda: pl.semaphore_wait(barrier, len(devices))


def remote(src, dst, send, recv, device):
    return pltpu.make_async_remote_copy(
        src_ref=src, dst_ref=dst, send_sem=send, recv_sem=recv,
        device_id=device, device_id_type=MESH,
    )


def tile_rows(labels, layout, ctx):
    n0 = jnp.int32(0)
    n1 = jnp.int32(0)
    for j in range(16):
        lab = labels[0, j]
        n0 = n0 + jnp.where(lab == 0, 1, 0)
        n1 = n1 + jnp.where(lab == 1, 1, 0)
    n2 = 16 - n0 - n1
    out = []
    for t in range(2):
        lab = labels[0, layout[0, 2 * ctx + t]]
        own = jnp.where(lab == 1, n1, jnp.where(lab == 2, n2, 0))
        count = ((n0 + own) * 128).astype(F32)
        out.append((lab, jnp.log(jnp.full((1, 128), count, F32))))
    return out


def dot_t(a, b):
    return lax.dot_general(a, b, (((1,), (1,)), ((), ())), preferred_element_type=F32)


def dot_n(a, b):
    return lax.dot_general(a, b, (((1,), (0,)), ((), ())), preferred_element_type=F32)


def dot_l(a, b):
    return lax.dot_general(a, b, (((0,), (0,)), ((), ())), preferred_element_type=F32)


ORDERS = ("xyz", "yzx", "zxy")
SIZES = {"l": 2, "x": 4, "y": 4, "h": 2}


def left_over(dims, axis):
    return "".join(d for d in dims if d not in ("lh" if axis == "z" else axis))


def block(dims, axis, coord):
    want = {"l": lax.rem(coord, 2), "h": coord // 2} if axis == "z" else {axis: coord}
    return tuple(want.get(d, slice(None)) for d in dims)


class Job:
    def __init__(self, n, j, part, refs, sems, here, device):
        self.chunk = 2 * n + j
        self.part = part.at[self.chunk]
        self.got1, self.comb, self.tot1, self.got2, self.tot2, self.got3 = refs
        self.send, self.recv = sems
        self.axes = ORDERS[n]
        self.dims = ["lxyh"]
        for axis in self.axes:
            self.dims.append(left_over(self.dims[-1], axis))
        self.at = [here[a] for a in self.axes]
        self.device = lambda stage, by: device(self.axes[stage], by)
        self.sent = []

    def go(self, sem, src, dst, device):
        c = remote(src, dst, self.send.at[sem], self.recv.at[sem], device)
        c.start()
        self.sent.append(c)

    def await_(self, sem, dst):
        remote(dst, dst, self.send.at[sem], self.recv.at[sem], self.device(0, 1)).wait_recv()

    def piece1(self, half, by):
        idx = block("lxyh", self.axes[0], lax.rem(self.at[0] + by, 4))
        return self.part.at[(half,) + idx]

    def start1(self):
        right, left = self.device(0, 1), self.device(0, -1)
        self.go(0, self.piece1(0, 2), self.got1.at[0], right)
        self.go(1, self.piece1(1, 2), self.got1.at[1], left)
        self.go(2, self.piece1(1, 1), self.got1.at[2], right)
        self.go(3, self.piece1(0, 3), self.got1.at[3], left)

    def combine(self):
        for m, by in ((0, 1), (1, 3)):
            self.await_(m, self.got1.at[m])
            mine = self.piece1(m, by)[...]
            self.comb[m] = (self.got1[m].astype(F32) + mine.astype(F32)).astype(BF16)
            self.go(4 + m, self.comb.at[m], self.got1.at[4 + m], self.device(0, 1 if m == 0 else -1))

    def finish1(self):
        for half, raw in ((0, 3), (1, 2)):
            self.await_(raw, self.got1.at[raw])
            self.await_(4 + half, self.got1.at[4 + half])
            total = self.piece1(half, 0)[...].astype(F32)
            total += self.got1[raw].astype(F32) + self.got1[4 + half].astype(F32)
            self.tot1[half] = total.astype(BF16)
        self.direct(1, self.tot1, self.got2, 6)

    def piece(self, stage, ref, by):
        idx = block(self.dims[stage], self.axes[stage], lax.rem(self.at[stage] + by, 4))
        return ref.at[(slice(None),) + idx]

    def direct(self, stage, ref, got, sem):
        for by in (2, 1, 3):
            self.go(sem + by - 1, self.piece(stage, ref, by), got.at[by - 1], self.device(stage, by))

    def summed(self, stage, ref, got, sem):
        total = self.piece(stage, ref, 0)[...].astype(F32)
        for by in (1, 3, 2):
            self.await_(sem + by - 1, got.at[by - 1])
            total += got[by - 1].astype(F32)
        return total

    def finish2(self):
        self.tot2[...] = self.summed(1, self.tot1, self.got2, 6).astype(BF16)
        self.direct(2, self.tot2, self.got3, 9)

    def finish3(self, out):
        total = self.summed(2, self.tot2, self.got3, 9)
        for half in range(2):
            at = self.chunk * 256 + half * 128
            out[:, at : at + 128] = total[half]

    def drain(self):
        for c in self.sent:
            c.wait_send()


def solve_kernel(
    labels, layout, lse, do_v, o_v, x_v, q, k, v, do,
    g_out, w_out,
    aux, lab8, labo, xt, xother, ko, vo, qo, doo, auxo, dk_acc, dv_acc, p_s, ds_s,
    dk_b, dv_b, dq_own, dq_give, dq_got, dq_sum, g, part,
    send, recv, fsend, frecv, xsem, dsend, drecv, osend, orecv, gsend, grecv, rsend, rrecv,
    *bufs,
):
    core, x, y, z_lo, z_hi, dp, ctx = place()
    here = {"x": x, "y": y, "z": z_hi * 2 + z_lo}
    sibling = (dp + 1 - 2 * core, ctx)

    def device(axis, by):
        c = dict(here)
        c[axis] = lax.rem(c[axis] + by + 4, 4)
        return (lax.rem(c["z"], 2) * 8 + c["x"] * 2 + core, c["y"] * 2 + c["z"] // 2)

    ready = greet(
        [target(h) for h in range(4)]
        + [owner(s) for s in range(4)]
        + [sibling]
        + [device(a, by) for a in "xyz" for by in (1, 2, 3)]
    )

    tiles = tile_rows(labels, layout, ctx)
    labs = jnp.concatenate(
        [jnp.full((1, 128), lab, jnp.int32) for lab, _ in tiles], axis=1
    )
    logs = jnp.concatenate([lg for _, lg in tiles], axis=1)
    for h in range(HEADS):
        cols = slice(h * HD, (h + 1) * HD)
        prod = do_v[0, :, cols].astype(F32) * o_v[0, :, cols].astype(F32)
        delta = jnp.sum(prod.T, axis=0, keepdims=True)
        ln = (logs + lse[0, h : h + 1, :]) * LOG2E
        aux[h, 0:1, :] = ln
        aux[h, 1:2, :] = jnp.where(labs == 1, ln, HIDDEN)
        aux[h, 2:3, :] = jnp.where(labs == 2, ln, HIDDEN)
        aux[h, 3:4, :] = delta
        aux[h, 4:8, :] = jnp.zeros((4, TOK), F32)
    lab8[...] = jnp.broadcast_to(labs.astype(F32), (8, TOK))

    def turn(dst, which):
        def one(i, carry):
            at = pl.multiple_of((2 * i + which) * 256, 256)
            dst[i] = x_v[0, :, pl.ds(at, 256)].T
            return carry

        lax.fori_loop(0, 8, one, 0)

    turn(xother, 1 - core)
    dk_acc[...] = jnp.zeros_like(dk_acc)
    dv_acc[...] = jnp.zeros_like(dv_acc)
    ready()

    hops = (0, 1, 3, 2)
    arrays = ((k, ko), (v, vo), (q, qo), (do, doo), (aux, auxo), (lab8, labo))
    sends = []
    for group in ((5, 0, 1), (4, 2, 3)):
        for t in hops:
            h = lax.rem(y + t, 4)
            for n in group:
                src, dst = arrays[n]
                if n == 5:
                    piece = src
                elif n == 4:
                    piece = src.at[h]
                else:
                    piece = src.at[0, :, pl.ds(pl.multiple_of(h * HD, HD), HD)]
                c = remote(piece, dst.at[y], send.at[n, t], recv.at[n, y], target(h))
                c.start()
                sends.append(c)
    cross = remote(xother, xt.at[1], xsem.at[0], xsem.at[1], sibling)
    cross.start()
    turn(xt.at[0], core)

    def arrived(ref, sem):
        remote(ref, ref, send.at[0, 0], sem, sibling).wait_recv()

    def left(ref, sem):
        remote(ref, ref, sem, recv.at[0, 0], sibling).wait_send()

    def slot(i):
        return lax.rem(y + jnp.where(i == 0, 0, jnp.where(i == 1, 3, i - 1)), 4)

    for t in (0, 3, 1, 2):
        s = lax.rem(y + t, 4)
        for n in (5, 0, 1):
            arrived(arrays[n][1].at[s], recv.at[n, s])

    def attend(c):
        k_all = ko[...].reshape(4 * TOK, HD)
        v_all = vo[...].reshape(4 * TOK, HD)
        qc = qo[c]
        doc = doo[c]
        s = dot_t(k_all, qc)
        d = dot_t(v_all, doc)
        rows = auxo[c]
        delta = rows[3:4, :]
        for t in range(8):
            part_ = slice(t * 128, (t + 1) * 128)
            at = (t % 2) * 128
            lab = labo[t // 2, 0:1, at : at + 1]
            row = jnp.where(
                lab == 0.0, rows[0:1, :], jnp.where(lab == 1.0, rows[1:2, :], rows[2:3, :])
            )
            p = jnp.exp2(s[part_] * (SCALE * LOG2E) - row)
            p_s[part_, :] = p.astype(BF16)
            ds_s[part_, :] = (p * (d[part_] - delta) * SCALE).astype(BF16)
        p_b = p_s[...]
        ds_b = ds_s[...]
        dv_acc[...] += dot_n(p_b, doc)
        dk_acc[...] += dot_n(ds_b, qc)
        return dot_l(ds_b, k_all)

    def hand_over(i):
        s = slot(i)
        arrived(dq_got.at[s], drecv.at[s])
        dq_sum[s] = (dq_own[s] + dq_got[s].astype(F32)).astype(BF16)
        remote(dq_sum.at[s], g.at[0, 0, y], osend.at[0, s], orecv.at[0, y], owner(s)).start()

    def step(i, carry):
        s = slot(i)
        for n in (4, 2, 3):
            dst = arrays[n][1]
            arrived(dst.at[s], recv.at[n, s])
            remote(dst.at[s], dst.at[4 + s], fsend.at[n - 2, s], frecv.at[n - 2, s], sibling).start()
        dq_own[s] = attend(s)

        @pl.when(i > 0)
        def _():
            hand_over(i - 1)

        for n in (4, 2, 3):
            arrived(arrays[n][1].at[4 + s], frecv.at[n - 2, s])
        dq_give[s] = attend(4 + s).astype(BF16)
        remote(dq_give.at[s], dq_got.at[s], dsend.at[s], drecv.at[s], sibling).start()
        return carry

    lax.fori_loop(0, 4, step, 0)
    for n, acc, buf in ((2, dv_acc, dv_b), (1, dk_acc, dk_b)):
        buf[...] = acc[...].astype(BF16).reshape(4, TOK, HD)
        for t in (2, 1, 3, 0):
            s = lax.rem(y + t, 4)
            remote(buf.at[s], g.at[0, n, y], osend.at[n, s], orecv.at[n, y], owner(s)).start()
    hand_over(3)

    def relay(n):
        for t in (0, 1, 3, 2):
            h = lax.rem(y + t, 4)
            arrived(g.at[0, n, h], orecv.at[n, h])
            remote(g.at[0, n, h], g.at[1, n, h], gsend.at[n, h], grecv.at[n, h], sibling).start()

    def whole(n):
        for h in range(4):
            arrived(g.at[1, n, h], grecv.at[n, h])

    jobs = {}
    for n in range(3):
        for j in range(2):
            c = 2 * n + j
            jobs[n, j] = Job(
                n, j, part, bufs[6 * c : 6 * c + 6], (rsend.at[c], rrecv.at[c]), here, device
            )

    def gemm(n, j):
        rhs = jnp.concatenate(
            [jnp.concatenate([g[c, n, 2 * j], g[c, n, 2 * j + 1]], axis=1) for c in range(2)], axis=0
        )

        def rows(i, carry):
            lhs = jnp.concatenate([xt[0, i], xt[1, i]], axis=1)
            res = dot_n(lhs, rhs).astype(BF16)
            for half in range(2):
                part[2 * n + j, half, i // 4, lax.rem(i, 4)] = res[
                    :, half * 128 : (half + 1) * 128
                ].reshape(4, 2, 32, 128)
            return carry

        lax.fori_loop(0, 8, rows, 0)

    cross.wait()
    order = (2, 1, 0)
    relay(2)
    relay(1)
    whole(2)
    gemm(2, 0)
    jobs[2, 0].start1()
    relay(0)
    whole(1)
    gemm(1, 0)
    jobs[1, 0].start1()
    whole(0)
    gemm(0, 0)
    jobs[0, 0].start1()
    for n in order:
        gemm(n, 1)
    for n in order:
        jobs[n, 0].combine()
        jobs[n, 1].start1()
    for n in order:
        jobs[n, 0].finish1()
    g_out[...] = g[0]
    for n in order:
        jobs[n, 1].combine()
    for n in order:
        jobs[n, 0].finish2()
    for n in order:
        jobs[n, 1].finish1()
    for n in order:
        jobs[n, 0].finish3(w_out)
    for n in order:
        jobs[n, 1].finish2()
    for n in order:
        jobs[n, 1].finish3(w_out)

    for job in jobs.values():
        job.drain()
    for c in sends:
        c.wait_send()
    for s in range(4):
        for n in (2, 3, 4):
            left(arrays[n][1].at[s], fsend.at[n - 2, s])
        left(dq_give.at[s], dsend.at[s])
        for n in range(3):
            left(dq_sum.at[s], osend.at[n, s])
            left(g.at[0, n, s], gsend.at[n, s])


def solve(labels, layout, lse, q, k, v, o, do, x_in):
    blk = lambda *n: pltpu.VMEM((*n, TOK, HD), BF16)
    sem = lambda *n: pltpu.SemaphoreType.DMA(n)
    scratch = [
        pltpu.VMEM((4, 8, TOK), F32),
        pltpu.VMEM((8, TOK), F32),
        pltpu.VMEM((4, 8, TOK), F32),
        pltpu.VMEM((2, 8, 256, TOK), BF16),
        pltpu.VMEM((8, 256, TOK), BF16),
        blk(4), blk(4), blk(8), blk(8),
        pltpu.VMEM((8, 8, TOK), F32),
        pltpu.VMEM((1024, HD), F32),
        pltpu.VMEM((1024, HD), F32),
        pltpu.VMEM((1024, TOK), BF16),
        pltpu.VMEM((1024, TOK), BF16),
        blk(4), blk(4),
        pltpu.VMEM((4, TOK, HD), F32),
        blk(4), blk(4), blk(4),
        blk(2, 3, 4),
        pltpu.VMEM((6, 2, 2, 4, 4, 2, 32, 128), BF16),
        sem(6, 4), sem(6, 4), sem(3, 4), sem(3, 4), sem(2), sem(4), sem(4),
        sem(3, 4), sem(3, 4), sem(3, 4), sem(3, 4), sem(6, 12), sem(6, 12),
    ]
    for n in range(3):
        for j in range(2):
            dims = ["lxyh"]
            for axis in ORDERS[n]:
                dims.append(left_over(dims[-1], axis))
            s1, s2, s3 = [tuple(SIZES[d] for d in ds) + (32, 128) for ds in dims[1:]]
            for shape in ((6,) + s1, (2,) + s1, (2,) + s1, (3, 2) + s2, (2,) + s2, (3, 2) + s3):
                scratch.append(pltpu.VMEM(shape, BF16))
    return pl.pallas_call(
        solve_kernel,
        out_shape=(
            jax.ShapeDtypeStruct((3, 4, TOK, HD), BF16),
            jax.ShapeDtypeStruct((32, 1536), F32),
        ),
        in_specs=[SM, SM, VM, VM, VM, VM, ANY, ANY, ANY, ANY],
        out_specs=(VM, VM),
        scratch_shapes=scratch,
        compiler_params=pltpu.CompilerParams(collective_id=0, has_side_effects=True),
        name="solve",
    )(labels, layout, lse, do, o, x_in, q, k, v, do)


def finish_kernel(g, w, gq, gk, gv, gw):
    for t, out in enumerate((gq, gk, gv)):
        for h in range(4):
            out[0, :, h * HD : (h + 1) * HD] = g[t, h]
    gw[...] = w[...]


def finish(g, w):
    grad = jax.ShapeDtypeStruct((1, TOK, HEADS * HD), BF16)
    return pl.pallas_call(
        finish_kernel,
        out_shape=(grad, grad, grad, jax.ShapeDtypeStruct(w.shape, w.dtype)),
        in_specs=[VM, VM],
        out_specs=(VM,) * 4,
        name="finish",
    )(g, w)


def per_device(inputs, queries, keys, values, attn_out, grad_out, lse_shift, labels, layout):
    g, w = solve(labels, layout, lse_shift, queries, keys, values, attn_out, grad_out, inputs)
    return finish(g, w)


def solution(mesh):
    tok = P("dp", "ctx", None)
    return jax.shard_map(
        per_device,
        mesh=mesh,
        in_specs=(tok,) * 6 + (P("dp", None, "ctx"), P("dp", None), P("dp", None)),
        out_specs=(tok, tok, tok, P(("dp", "ctx"), None)),
        check_vma=False,
    )
```

```python
import functools
import math

import jax
import jax.numpy as jnp
from jax import lax
from jax.experimental import pallas as pl
from jax.experimental.pallas import tpu as pltpu
from jax.sharding import PartitionSpec as P

HEADS = 4
HD = 128
TOK = 256
LOG2E = math.log2(math.e)
SCALE = 1.0 / math.sqrt(HD)
HIDDEN = 1e30
MESH = pl.DeviceIdType.MESH
F32 = jnp.float32
BF16 = jnp.bfloat16
ANY = pl.BlockSpec(memory_space=pl.ANY)
VM = pl.BlockSpec(memory_space=pltpu.VMEM)
SM = pl.BlockSpec(memory_space=pltpu.SMEM)


def place():
    dp = lax.axis_index("dp")
    ctx = lax.axis_index("ctx")
    core = lax.rem(dp, 2)
    x = lax.rem(dp // 2, 4)
    z_lo = dp // 8
    y = ctx // 2
    z_hi = lax.rem(ctx, 2)
    return core, x, y, z_lo, z_hi, dp, ctx


def flip(a, b):
    return lax.rem(a + b, 2)


def target(h):
    core, x, y, z_lo, z_hi, dp, ctx = place()
    return (dp - core + flip(1 + z_hi, y), h * 2 + flip(core, h))


def owner(s):
    core, x, y, z_lo, z_hi, dp, ctx = place()
    return (dp - core + flip(z_hi, y), s * 2 + flip(1 + core, s))


def greet(devices):
    barrier = pltpu.get_barrier_semaphore()
    for d in devices:
        pl.semaphore_signal(barrier, inc=1, device_id=d, device_id_type=MESH)
    return lambda: pl.semaphore_wait(barrier, len(devices))


def remote(src, dst, send, recv, device):
    return pltpu.make_async_remote_copy(
        src_ref=src, dst_ref=dst, send_sem=send, recv_sem=recv,
        device_id=device, device_id_type=MESH,
    )


def tile_rows(labels, layout, ctx):
    n0 = jnp.int32(0)
    n1 = jnp.int32(0)
    for j in range(16):
        lab = labels[0, j]
        n0 = n0 + jnp.where(lab == 0, 1, 0)
        n1 = n1 + jnp.where(lab == 1, 1, 0)
    n2 = 16 - n0 - n1
    out = []
    for t in range(2):
        lab = labels[0, layout[0, 2 * ctx + t]]
        own = jnp.where(lab == 1, n1, jnp.where(lab == 2, n2, 0))
        count = ((n0 + own) * 128).astype(F32)
        out.append((lab, jnp.log(jnp.full((1, 128), count, F32))))
    return out


def dot_t(a, b):
    return lax.dot_general(a, b, (((1,), (1,)), ((), ())), preferred_element_type=F32)


def dot_n(a, b):
    return lax.dot_general(a, b, (((1,), (0,)), ((), ())), preferred_element_type=F32)


def dot_l(a, b):
    return lax.dot_general(a, b, (((0,), (0,)), ((), ())), preferred_element_type=F32)


ORDERS = ("zxy", "yzx", "xyz")
SIZES = {"l": 2, "x": 4, "y": 4, "h": 2}


def left_over(dims, axis):
    return "".join(d for d in dims if d not in ("lh" if axis == "z" else axis))


def block(dims, axis, coord):
    want = {"l": lax.rem(coord, 2), "h": coord // 2} if axis == "z" else {axis: coord}
    return tuple(want.get(d, slice(None)) for d in dims)


class Job:
    def __init__(self, n, j, part, refs, sems, here, device):
        self.chunk = 2 * n + j
        self.part = part.at[self.chunk]
        self.got1, self.comb, self.tot1, self.got2, self.tot2, self.got3 = refs
        self.send, self.recv = sems
        self.axes = ORDERS[n]
        self.dims = ["lxyh"]
        for axis in self.axes:
            self.dims.append(left_over(self.dims[-1], axis))
        self.at = [here[a] for a in self.axes]
        self.device = lambda stage, by: device(self.axes[stage], by)
        self.sent = []

    def go(self, sem, src, dst, device):
        c = remote(src, dst, self.send.at[sem], self.recv.at[sem], device)
        c.start()
        self.sent.append(c)

    def await_(self, sem, dst):
        remote(dst, dst, self.send.at[sem], self.recv.at[sem], self.device(0, 1)).wait_recv()

    def piece1(self, half, by):
        idx = block("lxyh", self.axes[0], lax.rem(self.at[0] + by, 4))
        return self.part.at[(half,) + idx]

    def start1(self):
        right, left = self.device(0, 1), self.device(0, -1)
        self.go(0, self.piece1(0, 2), self.got1.at[0], right)
        self.go(1, self.piece1(1, 2), self.got1.at[1], left)
        self.go(2, self.piece1(1, 1), self.got1.at[2], right)
        self.go(3, self.piece1(0, 3), self.got1.at[3], left)

    def combine(self):
        for m, by in ((0, 1), (1, 3)):
            self.await_(m, self.got1.at[m])
            mine = self.piece1(m, by)[...]
            self.comb[m] = (self.got1[m].astype(F32) + mine.astype(F32)).astype(BF16)
            self.go(4 + m, self.comb.at[m], self.got1.at[4 + m], self.device(0, 1 if m == 0 else -1))

    def finish1(self):
        for half, raw in ((0, 3), (1, 2)):
            self.await_(raw, self.got1.at[raw])
            self.await_(4 + half, self.got1.at[4 + half])
            total = self.piece1(half, 0)[...].astype(F32)
            total += self.got1[raw].astype(F32) + self.got1[4 + half].astype(F32)
            self.tot1[half] = total.astype(BF16)
        self.direct(1, self.tot1, self.got2, 6)

    def piece(self, stage, ref, by):
        idx = block(self.dims[stage], self.axes[stage], lax.rem(self.at[stage] + by, 4))
        return ref.at[(slice(None),) + idx]

    def direct(self, stage, ref, got, sem):
        for by in (2, 1, 3):
            self.go(sem + by - 1, self.piece(stage, ref, by), got.at[by - 1], self.device(stage, by))

    def summed(self, stage, ref, got, sem):
        total = self.piece(stage, ref, 0)[...].astype(F32)
        for by in (1, 3, 2):
            self.await_(sem + by - 1, got.at[by - 1])
            total += got[by - 1].astype(F32)
        return total

    def finish2(self):
        self.tot2[...] = self.summed(1, self.tot1, self.got2, 6).astype(BF16)
        self.direct(2, self.tot2, self.got3, 9)

    def finish3(self, out):
        total = self.summed(2, self.tot2, self.got3, 9)
        for half in range(2):
            at = self.chunk * 256 + half * 128
            out[:, at : at + 128] = total[half]

    def drain(self):
        for c in self.sent:
            c.wait_send()


def solve_kernel(
    labels_hbm, layout_hbm, lse_hbm, x_hbm, o, q, k, v, do,
    g_out, w_out,
    labels, layout, lse, do_v, o_v, x_v, load,
    aux, lab8, labo, xt, xother, ko, vo, qo, doo, auxo, dq_acc, p_s, ds_s,
    dk_b, dv_b, dq_give, dq_got, dq_sum, g, part,
    send, recv, fsend, frecv, xsem, dsend, drecv, osend, orecv, gsend, grecv, rsend, rrecv,
    *bufs,
):
    core, x, y, z_lo, z_hi, dp, ctx = place()
    here = {"x": x, "y": y, "z": z_hi * 2 + z_lo}
    sibling = (dp + 1 - 2 * core, ctx)

    def device(axis, by):
        c = dict(here)
        c[axis] = lax.rem(c[axis] + by + 4, 4)
        return (lax.rem(c["z"], 2) * 8 + c["x"] * 2 + core, c["y"] * 2 + c["z"] // 2)

    ready = greet(
        [target(h) for h in range(4)]
        + [owner(s) for s in range(4)]
        + [sibling]
        + [device(a, by) for a in "xyz" for by in (1, 2, 3)]
    )

    loads = [
        pltpu.make_async_copy(src, dst, load.at[i])
        for i, (src, dst) in enumerate(
            ((labels_hbm, labels), (layout_hbm, layout), (lse_hbm, lse), (do, do_v), (o, o_v), (x_hbm, x_v))
        )
    ]
    for c in loads:
        c.start()
    ready()

    hops = (2, 1, 3, 0)
    arrays = ((k, ko), (v, vo), (q, qo), (do, doo), (aux, auxo), (lab8, labo))
    sends = []

    def give(n, t):
        h = lax.rem(y + t, 4)
        src, dst = arrays[n]
        if n == 5:
            piece = src
        elif n == 4:
            piece = src.at[h]
        else:
            piece = src.at[0, :, pl.ds(pl.multiple_of(h * HD, HD), HD)]
        c = remote(piece, dst.at[y], send.at[n, t], recv.at[n, y], target(h))
        c.start()
        sends.append(c)

    for t in hops:
        give(2, t)
        give(3, t)
    for c in loads[:5]:
        c.wait()
    tiles = tile_rows(labels, layout, ctx)
    labs = jnp.concatenate(
        [jnp.full((1, 128), lab, jnp.int32) for lab, _ in tiles], axis=1
    )
    logs = jnp.concatenate([lg for _, lg in tiles], axis=1)
    for h in range(HEADS):
        cols = slice(h * HD, (h + 1) * HD)
        prod = do_v[0, :, cols].astype(F32) * o_v[0, :, cols].astype(F32)
        delta = jnp.sum(prod.T, axis=0, keepdims=True)
        ln = (logs + lse[0, h : h + 1, :]) * LOG2E
        aux[h, 0:1, :] = ln
        aux[h, 1:2, :] = jnp.where(labs == 1, ln, HIDDEN)
        aux[h, 2:3, :] = jnp.where(labs == 2, ln, HIDDEN)
        aux[h, 3:4, :] = delta
        aux[h, 4:8, :] = jnp.zeros((4, TOK), F32)
    lab8[...] = jnp.broadcast_to(labs.astype(F32), (8, TOK))

    for t in hops:
        give(4, t)
    for t in hops:
        give(5, t)
        give(0, t)
        give(1, t)

    def turn(dst, which):
        def one(i, carry):
            at = pl.multiple_of((2 * i + which) * 256, 256)
            dst[i] = x_v[0, :, pl.ds(at, 256)].T
            return carry

        lax.fori_loop(0, 8, one, 0)

    loads[5].wait()
    turn(xother, 1 - core)
    cross = remote(xother, xt.at[1], xsem.at[0], xsem.at[1], sibling)
    cross.start()
    turn(xt.at[0], core)
    dq_acc[...] = jnp.zeros_like(dq_acc)

    def arrived(ref, sem):
        remote(ref, ref, send.at[0, 0], sem, sibling).wait_recv()

    def left(ref, sem):
        remote(ref, ref, sem, recv.at[0, 0], sibling).wait_send()

    def slot(i):
        return lax.rem(y + jnp.where(i == 0, 2, jnp.where(i == 1, 3, 3 - i)), 4)

    near = (2, 3, 1, 0)
    for t in near:
        s = lax.rem(y + t, 4)
        for n in (2, 3, 4):
            dst = arrays[n][1]
            arrived(dst.at[s], recv.at[n, s])
            remote(dst.at[s], dst.at[4 + s], fsend.at[n - 2, s], frecv.at[n - 2, s], sibling).start()
    for t in near:
        s = lax.rem(y + t, 4)
        for n in (2, 3, 4):
            arrived(arrays[n][1].at[4 + s], frecv.at[n - 2, s])

    def keys(i, carry):
        s = slot(i)
        for n in (5, 0, 1):
            arrived(arrays[n][1].at[s], recv.at[n, s])
        k_b = ko[s]
        v_b = vo[s]
        for c in range(4):
            pair = slice(2 * c, 2 * c + 2)
            sc = dot_t(k_b, qo[pair].reshape(2 * TOK, HD))
            dp_ = dot_t(v_b, doo[pair].reshape(2 * TOK, HD))
            rows = jnp.concatenate([auxo[2 * c], auxo[2 * c + 1]], axis=1)
            delta = rows[3:4, :]
            cols = slice(c * 2 * TOK, (c + 1) * 2 * TOK)
            for t in range(2):
                part_ = slice(t * 128, (t + 1) * 128)
                lab = labo[s, 0:1, t * 128 : t * 128 + 1]
                row = jnp.where(
                    lab == 0.0, rows[0:1, :], jnp.where(lab == 1.0, rows[1:2, :], rows[2:3, :])
                )
                p = jnp.exp2(sc[part_] * (SCALE * LOG2E) - row)
                p_s[part_, cols] = p.astype(BF16)
                ds_s[part_, cols] = (p * (dp_[part_] - delta) * SCALE).astype(BF16)
        q_all = qo[...].reshape(8 * TOK, HD)
        do_all = doo[...].reshape(8 * TOK, HD)
        dv_b[s] = dot_n(p_s[...], do_all).astype(BF16)
        remote(dv_b.at[s], g.at[0, 2, y], osend.at[2, s], orecv.at[2, y], owner(s)).start()
        dk_b[s] = dot_n(ds_s[...], q_all).astype(BF16)
        remote(dk_b.at[s], g.at[0, 1, y], osend.at[1, s], orecv.at[1, y], owner(s)).start()
        dq_acc[...] += dot_l(ds_s[...], k_b).reshape(8, TOK, HD)
        return carry

    lax.fori_loop(0, 4, keys, 0)
    for t in (2, 3, 1, 0):
        s = lax.rem(y + t, 4)
        dq_give[s] = dq_acc[4 + s].astype(BF16)
        remote(dq_give.at[s], dq_got.at[s], dsend.at[s], drecv.at[s], sibling).start()
    for t in (2, 3, 1, 0):
        s = lax.rem(y + t, 4)
        arrived(dq_got.at[s], drecv.at[s])
        dq_sum[s] = (dq_acc[s] + dq_got[s].astype(F32)).astype(BF16)
        remote(dq_sum.at[s], g.at[0, 0, y], osend.at[0, s], orecv.at[0, y], owner(s)).start()

    def relay(*parts):
        for t, n in ((t, n) for t in (2, 1, 3, 0) for n in parts):
            h = lax.rem(y + t, 4)
            arrived(g.at[0, n, h], orecv.at[n, h])
            remote(g.at[0, n, h], g.at[1, n, h], gsend.at[n, h], grecv.at[n, h], sibling).start()

    def whole(n):
        for h in range(4):
            arrived(g.at[1, n, h], grecv.at[n, h])

    jobs = {}
    for n in range(3):
        for j in range(2):
            c = 2 * n + j
            jobs[n, j] = Job(
                n, j, part, bufs[6 * c : 6 * c + 6], (rsend.at[c], rrecv.at[c]), here, device
            )

    def gemm(n, j):
        rhs = jnp.concatenate(
            [jnp.concatenate([g[c, n, 2 * j], g[c, n, 2 * j + 1]], axis=1) for c in range(2)], axis=0
        )

        def rows(i, carry):
            lhs = jnp.concatenate(
                [xt[c, pl.ds(i * 4, 4)].reshape(1024, TOK) for c in range(2)], axis=1
            )
            res = dot_n(lhs, rhs).astype(BF16)
            for half in range(2):
                part[2 * n + j, half, i] = res[:, half * 128 : (half + 1) * 128].reshape(
                    4, 4, 2, 32, 128
                )
            return carry

        lax.fori_loop(0, 2, rows, 0)

    cross.wait()
    order = (2, 1, 0)
    relay(2, 1)
    whole(2)
    gemm(2, 0)
    jobs[2, 0].start1()
    relay(0)
    whole(1)
    gemm(1, 0)
    jobs[1, 0].start1()
    whole(0)
    gemm(0, 0)
    jobs[0, 0].start1()
    for n in order:
        gemm(n, 1)
    for n in order:
        jobs[n, 0].combine()
        jobs[n, 1].start1()
    for n in order:
        jobs[n, 0].finish1()
    g_out[...] = g[0]
    for n in order:
        jobs[n, 1].combine()
    for n in order:
        jobs[n, 0].finish2()
    for n in order:
        jobs[n, 1].finish1()
    for n in order:
        jobs[n, 0].finish3(w_out)
    for n in order:
        jobs[n, 1].finish2()
    for n in order:
        jobs[n, 1].finish3(w_out)

    for job in jobs.values():
        job.drain()
    for c in sends:
        c.wait_send()
    for s in range(4):
        for n in (2, 3, 4):
            left(arrays[n][1].at[s], fsend.at[n - 2, s])
        left(dq_give.at[s], dsend.at[s])
        for n in range(3):
            left(dq_sum.at[s], osend.at[n, s])
            left(g.at[0, n, s], gsend.at[n, s])


def solve(labels, layout, lse, q, k, v, o, do, x_in):
    blk = lambda *n: pltpu.VMEM((*n, TOK, HD), BF16)
    sem = lambda *n: pltpu.SemaphoreType.DMA(n)
    scratch = [
        pltpu.SMEM((1, 16), jnp.int32),
        pltpu.SMEM((1, 16), jnp.int32),
        pltpu.VMEM((1, 4, TOK), F32),
        pltpu.VMEM((1, TOK, 512), BF16),
        pltpu.VMEM((1, TOK, 512), BF16),
        pltpu.VMEM((1, TOK, 4096), BF16),
        sem(6),
        pltpu.VMEM((4, 8, TOK), F32),
        pltpu.VMEM((8, TOK), F32),
        pltpu.VMEM((4, 8, TOK), F32),
        pltpu.VMEM((2, 8, 256, TOK), BF16),
        pltpu.VMEM((8, 256, TOK), BF16),
        blk(4), blk(4), blk(8), blk(8),
        pltpu.VMEM((8, 8, TOK), F32),
        pltpu.VMEM((8, TOK, HD), F32),
        pltpu.VMEM((TOK, 2048), BF16),
        pltpu.VMEM((TOK, 2048), BF16),
        blk(4), blk(4),
        blk(4), blk(4), blk(4),
        blk(2, 3, 4),
        pltpu.VMEM((6, 2, 2, 4, 4, 2, 32, 128), BF16),
        sem(6, 4), sem(6, 4), sem(3, 4), sem(3, 4), sem(2), sem(4), sem(4),
        sem(3, 4), sem(3, 4), sem(3, 4), sem(3, 4), sem(6, 12), sem(6, 12),
    ]
    for n in range(3):
        for j in range(2):
            dims = ["lxyh"]
            for axis in ORDERS[n]:
                dims.append(left_over(dims[-1], axis))
            s1, s2, s3 = [tuple(SIZES[d] for d in ds) + (32, 128) for ds in dims[1:]]
            for shape in ((6,) + s1, (2,) + s1, (2,) + s1, (3, 2) + s2, (2,) + s2, (3, 2) + s3):
                scratch.append(pltpu.VMEM(shape, BF16))
    return pl.pallas_call(
        solve_kernel,
        out_shape=(
            jax.ShapeDtypeStruct((3, 4, TOK, HD), BF16),
            jax.ShapeDtypeStruct((32, 1536), F32),
        ),
        in_specs=[ANY] * 9,
        out_specs=(VM, VM),
        scratch_shapes=scratch,
        compiler_params=pltpu.CompilerParams(collective_id=0, has_side_effects=True),
        name="solve",
    )(labels, layout, lse, x_in, o, q, k, v, do)


def finish_kernel(g, w, gq, gk, gv, gw):
    for t, out in enumerate((gq, gk, gv)):
        for h in range(4):
            out[0, :, h * HD : (h + 1) * HD] = g[t, h]
    gw[...] = w[...]


def finish(g, w):
    grad = jax.ShapeDtypeStruct((1, TOK, HEADS * HD), BF16)
    return pl.pallas_call(
        finish_kernel,
        out_shape=(grad, grad, grad, jax.ShapeDtypeStruct(w.shape, w.dtype)),
        in_specs=[VM, VM],
        out_specs=(VM,) * 4,
        name="finish",
    )(g, w)


def per_device(inputs, queries, keys, values, attn_out, grad_out, lse_shift, labels, layout):
    g, w = solve(labels, layout, lse_shift, queries, keys, values, attn_out, grad_out, inputs)
    return finish(g, w)


def solution(mesh):
    tok = P("dp", "ctx", None)
    return jax.shard_map(
        per_device,
        mesh=mesh,
        in_specs=(tok,) * 6 + (P("dp", None, "ctx"), P("dp", None), P("dp", None)),
        out_specs=(tok, tok, tok, P(("dp", "ctx"), None)),
        check_vma=False,
    )
```

```python
import functools
import math

import jax
import jax.numpy as jnp
from jax import lax
from jax.experimental import pallas as pl
from jax.experimental.pallas import tpu as pltpu
from jax.sharding import PartitionSpec as P

HEADS = 4
HD = 128
TOK = 256
LOG2E = math.log2(math.e)
SCALE = 1.0 / math.sqrt(HD)
HIDDEN = 1e30
MESH = pl.DeviceIdType.MESH
F32 = jnp.float32
BF16 = jnp.bfloat16
ANY = pl.BlockSpec(memory_space=pl.ANY)
VM = pl.BlockSpec(memory_space=pltpu.VMEM)
SM = pl.BlockSpec(memory_space=pltpu.SMEM)


def place():
    dp = lax.axis_index("dp")
    ctx = lax.axis_index("ctx")
    core = lax.rem(dp, 2)
    x = lax.rem(dp // 2, 4)
    z_lo = dp // 8
    y = ctx // 2
    z_hi = lax.rem(ctx, 2)
    return core, x, y, z_lo, z_hi, dp, ctx


def flip(a, b):
    return lax.rem(a + b, 2)


def target(h):
    core, x, y, z_lo, z_hi, dp, ctx = place()
    return (dp - core + flip(1 + z_hi, y), h * 2 + flip(core, h))


def owner(s):
    core, x, y, z_lo, z_hi, dp, ctx = place()
    return (dp - core + flip(z_hi, y), s * 2 + flip(1 + core, s))


def greet(devices):
    barrier = pltpu.get_barrier_semaphore()
    for d in devices:
        pl.semaphore_signal(barrier, inc=1, device_id=d, device_id_type=MESH)
    return lambda: pl.semaphore_wait(barrier, len(devices))


def remote(src, dst, send, recv, device):
    return pltpu.make_async_remote_copy(
        src_ref=src, dst_ref=dst, send_sem=send, recv_sem=recv,
        device_id=device, device_id_type=MESH,
    )


def tile_rows(labels, layout, ctx):
    n0 = jnp.int32(0)
    n1 = jnp.int32(0)
    for j in range(16):
        lab = labels[0, j]
        n0 = n0 + jnp.where(lab == 0, 1, 0)
        n1 = n1 + jnp.where(lab == 1, 1, 0)
    n2 = 16 - n0 - n1
    out = []
    for t in range(2):
        lab = labels[0, layout[0, 2 * ctx + t]]
        own = jnp.where(lab == 1, n1, jnp.where(lab == 2, n2, 0))
        count = ((n0 + own) * 128).astype(F32)
        out.append((lab, jnp.log(jnp.full((1, 128), count, F32))))
    return out


def dot_t(a, b):
    return lax.dot_general(a, b, (((1,), (1,)), ((), ())), preferred_element_type=F32)


def dot_n(a, b):
    return lax.dot_general(a, b, (((1,), (0,)), ((), ())), preferred_element_type=F32)


def dot_l(a, b):
    return lax.dot_general(a, b, (((0,), (0,)), ((), ())), preferred_element_type=F32)


ORDERS = ("xyz", "yzx", "zxy")
CHUNKS = ((2, 0), (2, 1), (1, 0), (1, 1), (0, 0), (0, 1))
SIZES = {"l": 2, "x": 4, "y": 4, "h": 2}


def left_over(dims, axis):
    return "".join(d for d in dims if d not in ("lh" if axis == "z" else axis))


def block(dims, axis, coord):
    want = {"l": lax.rem(coord, 2), "h": coord // 2} if axis == "z" else {axis: coord}
    return tuple(want.get(d, slice(None)) for d in dims)


class Job:
    def __init__(self, n, j, axes, part, refs, sems, here, device):
        self.chunk = 2 * n + j
        self.part = part.at[self.chunk]
        self.got1, self.comb, self.tot1, self.got2, self.tot2, self.got3 = refs
        self.send, self.recv = sems
        self.axes = axes
        self.dims = ["lxyh"]
        for axis in self.axes:
            self.dims.append(left_over(self.dims[-1], axis))
        self.at = [here[a] for a in self.axes]
        self.device = lambda stage, by: device(self.axes[stage], by)
        self.sent = []

    def go(self, sem, src, dst, device):
        c = remote(src, dst, self.send.at[sem], self.recv.at[sem], device)
        c.start()
        self.sent.append(c)

    def await_(self, sem, dst):
        remote(dst, dst, self.send.at[sem], self.recv.at[sem], self.device(0, 1)).wait_recv()

    def piece1(self, half, by):
        idx = block("lxyh", self.axes[0], lax.rem(self.at[0] + by, 4))
        return self.part.at[(half,) + idx]

    def start1(self):
        right, left = self.device(0, 1), self.device(0, -1)
        self.go(0, self.piece1(0, 2), self.got1.at[0], right)
        self.go(1, self.piece1(1, 2), self.got1.at[1], left)
        self.go(2, self.piece1(1, 1), self.got1.at[2], right)
        self.go(3, self.piece1(0, 3), self.got1.at[3], left)

    def combine(self):
        for m, by in ((0, 1), (1, 3)):
            self.await_(m, self.got1.at[m])
            mine = self.piece1(m, by)[...]
            self.comb[m] = (self.got1[m].astype(F32) + mine.astype(F32)).astype(BF16)
            self.go(4 + m, self.comb.at[m], self.got1.at[4 + m], self.device(0, 1 if m == 0 else -1))

    def finish1(self):
        for half, raw in ((0, 3), (1, 2)):
            self.await_(raw, self.got1.at[raw])
            self.await_(4 + half, self.got1.at[4 + half])
            total = self.piece1(half, 0)[...].astype(F32)
            total += self.got1[raw].astype(F32) + self.got1[4 + half].astype(F32)
            self.tot1[half] = total.astype(BF16)
        self.direct(1, self.tot1, self.got2, 6)

    def piece(self, stage, ref, by):
        idx = block(self.dims[stage], self.axes[stage], lax.rem(self.at[stage] + by, 4))
        return ref.at[(slice(None),) + idx]

    def direct(self, stage, ref, got, sem):
        for by in (2, 1, 3):
            self.go(sem + by - 1, self.piece(stage, ref, by), got.at[by - 1], self.device(stage, by))

    def summed(self, stage, ref, got, sem):
        total = self.piece(stage, ref, 0)[...].astype(F32)
        for by in (1, 3, 2):
            self.await_(sem + by - 1, got.at[by - 1])
            total += got[by - 1].astype(F32)
        return total

    def finish2(self):
        self.tot2[...] = self.summed(1, self.tot1, self.got2, 6).astype(BF16)
        self.direct(2, self.tot2, self.got3, 9)

    def finish3(self, out):
        total = self.summed(2, self.tot2, self.got3, 9)
        for half in range(2):
            at = self.chunk * 256 + half * 128
            out[:, at : at + 128] = total[half]

    def drain(self):
        for c in self.sent:
            c.wait_send()


def solve_kernel(
    labels_hbm, layout_hbm, lse_hbm, x_hbm, o, q, k, v, do,
    gq_out, gk_out, gv_out, w_out,
    labels, layout, lse, do_v, o_v, x_v, load, gout,
    aux, lab8, labo, xt, xother, ko, vo, qo, doo, auxo, dq_acc, p_s, ds_s,
    dk_b, dv_b, dq_give, dq_got, dq_sum, g, part,
    send, recv, fsend, frecv, xsem, dsend, drecv, osend, orecv, gsend, grecv, rsend, rrecv,
    *bufs,
):
    core, x, y, z_lo, z_hi, dp, ctx = place()
    here = {"x": x, "y": y, "z": z_hi * 2 + z_lo}
    sibling = (dp + 1 - 2 * core, ctx)

    def device(axis, by):
        c = dict(here)
        c[axis] = lax.rem(c[axis] + by + 4, 4)
        return (lax.rem(c["z"], 2) * 8 + c["x"] * 2 + core, c["y"] * 2 + c["z"] // 2)

    ready = greet(
        [target(h) for h in range(4)]
        + [owner(s) for s in range(4)]
        + [sibling]
        + [device(a, by) for a in "xyz" for by in (1, 2, 3)]
    )

    loads = [
        pltpu.make_async_copy(src, dst, load.at[i])
        for i, (src, dst) in enumerate(
            ((labels_hbm, labels), (layout_hbm, layout), (lse_hbm, lse), (do, do_v), (o, o_v), (x_hbm, x_v))
        )
    ]
    for c in loads:
        c.start()
    ready()

    hops = (1, 3, 2, 0)
    arrays = ((k, ko), (v, vo), (q, qo), (do, doo), (aux, auxo), (lab8, labo))
    sends = []

    def give(n, t):
        h = lax.rem(y + t, 4)
        src, dst = arrays[n]
        if n == 5:
            piece = src
        elif n == 4:
            piece = src.at[h]
        else:
            piece = src.at[0, :, pl.ds(pl.multiple_of(h * HD, HD), HD)]
        c = remote(piece, dst.at[y], send.at[n, t], recv.at[n, y], target(h))
        c.start()
        sends.append(c)

    for t in hops:
        give(2, t)
        give(3, t)
    for c in loads[:5]:
        c.wait()
    tiles = tile_rows(labels, layout, ctx)
    labs = jnp.concatenate(
        [jnp.full((1, 128), lab, jnp.int32) for lab, _ in tiles], axis=1
    )
    logs = jnp.concatenate([lg for _, lg in tiles], axis=1)
    for h in range(HEADS):
        cols = slice(h * HD, (h + 1) * HD)
        prod = do_v[0, :, cols].astype(F32) * o_v[0, :, cols].astype(F32)
        delta = jnp.sum(prod.T, axis=0, keepdims=True)
        ln = (logs + lse[0, h : h + 1, :]) * LOG2E
        aux[h, 0:1, :] = ln
        aux[h, 1:2, :] = jnp.where(labs == 1, ln, HIDDEN)
        aux[h, 2:3, :] = jnp.where(labs == 2, ln, HIDDEN)
        aux[h, 3:4, :] = delta
        aux[h, 4:8, :] = jnp.zeros((4, TOK), F32)
    lab8[...] = jnp.broadcast_to(labs.astype(F32), (8, TOK))

    for t in hops:
        give(4, t)
    for t in hops:
        give(5, t)
        give(0, t)
        give(1, t)

    def turn(dst, which):
        def one(i, carry):
            at = pl.multiple_of((2 * i + which) * 256, 256)
            dst[i] = x_v[0, :, pl.ds(at, 256)].T
            return carry

        lax.fori_loop(0, 8, one, 0)

    loads[5].wait()
    turn(xother, 1 - core)
    cross = remote(xother, xt.at[1], xsem.at[0], xsem.at[1], sibling)
    cross.start()
    turn(xt.at[0], core)
    dq_acc[...] = jnp.zeros_like(dq_acc)

    def arrived(ref, sem):
        remote(ref, ref, send.at[0, 0], sem, sibling).wait_recv()

    def left(ref, sem):
        remote(ref, ref, sem, recv.at[0, 0], sibling).wait_send()

    def slot(i):
        return lax.rem(y + jnp.where(i == 0, 3, jnp.where(i == 3, 0, i)), 4)

    near = (3, 1, 2, 0)
    for t in near:
        s = lax.rem(y + t, 4)
        for n in (2, 3, 4):
            dst = arrays[n][1]
            arrived(dst.at[s], recv.at[n, s])
            remote(dst.at[s], dst.at[4 + s], fsend.at[n - 2, s], frecv.at[n - 2, s], sibling).start()
    for t in near:
        s = lax.rem(y + t, 4)
        for n in (2, 3, 4):
            arrived(arrays[n][1].at[4 + s], frecv.at[n - 2, s])

    def keys(i, carry):
        s = slot(i)
        for n in (5, 0, 1):
            arrived(arrays[n][1].at[s], recv.at[n, s])
        k_b = ko[s]
        v_b = vo[s]
        for c in range(4):
            pair = slice(2 * c, 2 * c + 2)
            sc = dot_t(k_b, qo[pair].reshape(2 * TOK, HD))
            dp_ = dot_t(v_b, doo[pair].reshape(2 * TOK, HD))
            rows = jnp.concatenate([auxo[2 * c], auxo[2 * c + 1]], axis=1)
            delta = rows[3:4, :]
            cols = slice(c * 2 * TOK, (c + 1) * 2 * TOK)
            for t in range(2):
                part_ = slice(t * 128, (t + 1) * 128)
                lab = labo[s, 0:1, t * 128 : t * 128 + 1]
                row = jnp.where(
                    lab == 0.0, rows[0:1, :], jnp.where(lab == 1.0, rows[1:2, :], rows[2:3, :])
                )
                p = jnp.exp2(sc[part_] * (SCALE * LOG2E) - row)
                p_s[part_, cols] = p.astype(BF16)
                ds_s[part_, cols] = (p * (dp_[part_] - delta) * SCALE).astype(BF16)
        q_all = qo[...].reshape(8 * TOK, HD)
        do_all = doo[...].reshape(8 * TOK, HD)
        dv_b[s] = dot_n(p_s[...], do_all).astype(BF16)
        remote(dv_b.at[s], g.at[0, 2, y], osend.at[2, s], orecv.at[2, y], owner(s)).start()
        dk_b[s] = dot_n(ds_s[...], q_all).astype(BF16)
        remote(dk_b.at[s], g.at[0, 1, y], osend.at[1, s], orecv.at[1, y], owner(s)).start()
        dq_acc[...] += dot_l(ds_s[...], k_b).reshape(8, TOK, HD)
        return carry

    lax.fori_loop(0, 4, keys, 0)
    for t in (2, 3, 1, 0):
        s = lax.rem(y + t, 4)
        dq_give[s] = dq_acc[4 + s].astype(BF16)
        remote(dq_give.at[s], dq_got.at[s], dsend.at[s], drecv.at[s], sibling).start()
    for t in (2, 3, 1, 0):
        s = lax.rem(y + t, 4)
        arrived(dq_got.at[s], drecv.at[s])
        dq_sum[s] = (dq_acc[s] + dq_got[s].astype(F32)).astype(BF16)
        remote(dq_sum.at[s], g.at[0, 0, y], osend.at[0, s], orecv.at[0, y], owner(s)).start()

    def relay(*parts):
        for t, n in ((t, n) for t in (1, 3, 2, 0) for n in parts):
            h = lax.rem(y + t, 4)
            arrived(g.at[0, n, h], orecv.at[n, h])
            remote(g.at[0, n, h], g.at[1, n, h], gsend.at[n, h], grecv.at[n, h], sibling).start()

    def whole(n):
        for h in range(4):
            arrived(g.at[1, n, h], grecv.at[n, h])

    jobs = []
    for c, (n, j) in enumerate(CHUNKS):
        jobs.append(
            Job(
                n, j, ORDERS[c % 3], part, bufs[6 * c : 6 * c + 6],
                (rsend.at[c], rrecv.at[c]), here, device,
            )
        )

    def gemm(n, j):
        rhs = jnp.concatenate(
            [jnp.concatenate([g[c, n, 2 * j], g[c, n, 2 * j + 1]], axis=1) for c in range(2)], axis=0
        )

        def rows(i, carry):
            lhs = jnp.concatenate(
                [xt[c, pl.ds(i * 4, 4)].reshape(1024, TOK) for c in range(2)], axis=1
            )
            res = dot_n(lhs, rhs).astype(BF16)
            for half in range(2):
                part[2 * n + j, half, i] = res[:, half * 128 : (half + 1) * 128].reshape(
                    4, 4, 2, 32, 128
                )
            return carry

        lax.fori_loop(0, 2, rows, 0)

    cross.wait()
    first, second = jobs[:3], jobs[3:]
    relay(2, 1)
    whole(2)
    for c in range(2):
        gemm(*CHUNKS[c])
        first[c].start1()
    whole(1)
    gemm(*CHUNKS[2])
    first[2].start1()
    gemm(*CHUNKS[3])
    relay(0)
    whole(0)
    gemm(*CHUNKS[4])
    gemm(*CHUNKS[5])
    for one, two in zip(first, second):
        one.combine()
        two.start1()
    for one in first:
        one.finish1()
    outs = [
        pltpu.make_async_copy(g.at[0, n, h], dst.at[0, :, h * HD : (h + 1) * HD], gout.at[n, h])
        for n, dst in enumerate((gq_out, gk_out, gv_out))
        for h in range(HEADS)
    ]
    for c in outs:
        c.start()
    for two in second:
        two.combine()
    for one in first:
        one.finish2()
    for two in second:
        two.finish1()
    for one in first:
        one.finish3(w_out)
    for two in second:
        two.finish2()
    for two in second:
        two.finish3(w_out)

    for job in jobs:
        job.drain()
    for c in outs:
        c.wait()
    for c in sends:
        c.wait_send()
    for s in range(4):
        for n in (2, 3, 4):
            left(arrays[n][1].at[s], fsend.at[n - 2, s])
        left(dq_give.at[s], dsend.at[s])
        for n in range(3):
            left(dq_sum.at[s], osend.at[n, s])
            left(g.at[0, n, s], gsend.at[n, s])


def solve(labels, layout, lse, q, k, v, o, do, x_in):
    blk = lambda *n: pltpu.VMEM((*n, TOK, HD), BF16)
    sem = lambda *n: pltpu.SemaphoreType.DMA(n)
    scratch = [
        pltpu.SMEM((1, 16), jnp.int32),
        pltpu.SMEM((1, 16), jnp.int32),
        pltpu.VMEM((1, 4, TOK), F32),
        pltpu.VMEM((1, TOK, 512), BF16),
        pltpu.VMEM((1, TOK, 512), BF16),
        pltpu.VMEM((1, TOK, 4096), BF16),
        sem(6),
        sem(3, 4),
        pltpu.VMEM((4, 8, TOK), F32),
        pltpu.VMEM((8, TOK), F32),
        pltpu.VMEM((4, 8, TOK), F32),
        pltpu.VMEM((2, 8, 256, TOK), BF16),
        pltpu.VMEM((8, 256, TOK), BF16),
        blk(4), blk(4), blk(8), blk(8),
        pltpu.VMEM((8, 8, TOK), F32),
        pltpu.VMEM((8, TOK, HD), F32),
        pltpu.VMEM((TOK, 2048), BF16),
        pltpu.VMEM((TOK, 2048), BF16),
        blk(4), blk(4),
        blk(4), blk(4), blk(4),
        blk(2, 3, 4),
        pltpu.VMEM((6, 2, 2, 4, 4, 2, 32, 128), BF16),
        sem(6, 4), sem(6, 4), sem(3, 4), sem(3, 4), sem(2), sem(4), sem(4),
        sem(3, 4), sem(3, 4), sem(3, 4), sem(3, 4), sem(6, 12), sem(6, 12),
    ]
    for c in range(6):
        dims = ["lxyh"]
        for axis in ORDERS[c % 3]:
            dims.append(left_over(dims[-1], axis))
        s1, s2, s3 = [tuple(SIZES[d] for d in ds) + (32, 128) for ds in dims[1:]]
        for shape in ((6,) + s1, (2,) + s1, (2,) + s1, (3, 2) + s2, (2,) + s2, (3, 2) + s3):
            scratch.append(pltpu.VMEM(shape, BF16))
    return pl.pallas_call(
        solve_kernel,
        out_shape=(
            *(jax.ShapeDtypeStruct((1, TOK, HEADS * HD), BF16),) * 3,
            jax.ShapeDtypeStruct((32, 1536), F32),
        ),
        in_specs=[ANY] * 9,
        out_specs=(ANY, ANY, ANY, VM),
        scratch_shapes=scratch,
        compiler_params=pltpu.CompilerParams(collective_id=0, has_side_effects=True),
        name="solve",
    )(labels, layout, lse, x_in, o, q, k, v, do)


def finish_kernel(*refs):
    ins, outs, bufs = refs[:4], refs[4:8], refs[8:12]
    got, put = refs[12:]
    loads = [pltpu.make_async_copy(a, b, got.at[i]) for i, (a, b) in enumerate(zip(ins, bufs))]
    stores = [pltpu.make_async_copy(a, b, put.at[i]) for i, (a, b) in enumerate(zip(bufs, outs))]
    for c in loads:
        c.start()
    for a, b in zip(loads, stores):
        a.wait()
        b.start()
    for c in stores:
        c.wait()


def finish(*arrays):
    return pl.pallas_call(
        finish_kernel,
        out_shape=tuple(jax.ShapeDtypeStruct(a.shape, a.dtype) for a in arrays),
        in_specs=[ANY] * 4,
        out_specs=(ANY,) * 4,
        scratch_shapes=[pltpu.VMEM(a.shape, a.dtype) for a in arrays]
        + [pltpu.SemaphoreType.DMA((4,))] * 2,
        name="finish",
    )(*arrays)


def per_device(inputs, queries, keys, values, attn_out, grad_out, lse_shift, labels, layout):
    grads = solve(labels, layout, lse_shift, queries, keys, values, attn_out, grad_out, inputs)
    return finish(*grads)


def solution(mesh):
    tok = P("dp", "ctx", None)
    return jax.shard_map(
        per_device,
        mesh=mesh,
        in_specs=(tok,) * 6 + (P("dp", None, "ctx"), P("dp", None), P("dp", None)),
        out_specs=(tok, tok, tok, P(("dp", "ctx"), None)),
        check_vma=False,
    )
```

```python
import functools
import math

import jax
import jax.numpy as jnp
from jax import lax
from jax.experimental import pallas as pl
from jax.experimental.pallas import tpu as pltpu
from jax.sharding import PartitionSpec as P

HEADS = 4
HD = 128
TOK = 256
LOG2E = math.log2(math.e)
SCALE = 1.0 / math.sqrt(HD)
HIDDEN = 1e30
MESH = pl.DeviceIdType.MESH
F32 = jnp.float32
BF16 = jnp.bfloat16
ANY = pl.BlockSpec(memory_space=pl.ANY)
VM = pl.BlockSpec(memory_space=pltpu.VMEM)
SM = pl.BlockSpec(memory_space=pltpu.SMEM)


def place():
    dp = lax.axis_index("dp")
    ctx = lax.axis_index("ctx")
    core = lax.rem(dp, 2)
    x = lax.rem(dp // 2, 4)
    z_lo = dp // 8
    y = ctx // 2
    z_hi = lax.rem(ctx, 2)
    return core, x, y, z_lo, z_hi, dp, ctx


def flip(a, b):
    return lax.rem(a + b, 2)


def target(h):
    core, x, y, z_lo, z_hi, dp, ctx = place()
    return (dp - core + flip(1 + z_hi, y), h * 2 + flip(core, h))


def owner(s):
    core, x, y, z_lo, z_hi, dp, ctx = place()
    return (dp - core + flip(z_hi, y), s * 2 + flip(1 + core, s))


def greet(devices):
    barrier = pltpu.get_barrier_semaphore()
    for d in devices:
        pl.semaphore_signal(barrier, inc=1, device_id=d, device_id_type=MESH)
    return lambda: pl.semaphore_wait(barrier, len(devices))


def remote(src, dst, send, recv, device):
    return pltpu.make_async_remote_copy(
        src_ref=src, dst_ref=dst, send_sem=send, recv_sem=recv,
        device_id=device, device_id_type=MESH,
    )


def tile_rows(labels, layout, ctx):
    n0 = jnp.int32(0)
    n1 = jnp.int32(0)
    for j in range(16):
        lab = labels[0, j]
        n0 = n0 + jnp.where(lab == 0, 1, 0)
        n1 = n1 + jnp.where(lab == 1, 1, 0)
    n2 = 16 - n0 - n1
    out = []
    for t in range(2):
        lab = labels[0, layout[0, 2 * ctx + t]]
        own = jnp.where(lab == 1, n1, jnp.where(lab == 2, n2, 0))
        count = ((n0 + own) * 128).astype(F32)
        out.append((lab, jnp.log(jnp.full((1, 128), count, F32))))
    return out


def dot_t(a, b):
    return lax.dot_general(a, b, (((1,), (1,)), ((), ())), preferred_element_type=F32)


def dot_n(a, b):
    return lax.dot_general(a, b, (((1,), (0,)), ((), ())), preferred_element_type=F32)


def dot_l(a, b):
    return lax.dot_general(a, b, (((0,), (0,)), ((), ())), preferred_element_type=F32)


ORDERS = ("xyz", "yzx", "zxy")
CHUNKS = ((2, 0), (2, 1), (1, 0), (1, 1), (0, 0), (0, 1))
SIZES = {"l": 2, "x": 4, "y": 4, "h": 2}


def left_over(dims, axis):
    return "".join(d for d in dims if d not in ("lh" if axis == "z" else axis))


def block(dims, axis, coord):
    want = {"l": lax.rem(coord, 2), "h": coord // 2} if axis == "z" else {axis: coord}
    return tuple(want.get(d, slice(None)) for d in dims)


class Job:
    def __init__(self, n, j, axes, part, refs, sems, here, device):
        self.chunk = 2 * n + j
        self.part = part.at[self.chunk]
        self.got1, self.comb, self.tot1, self.got2, self.tot2, self.got3 = refs
        self.send, self.recv = sems
        self.axes = axes
        self.dims = ["lxyh"]
        for axis in self.axes:
            self.dims.append(left_over(self.dims[-1], axis))
        self.at = [here[a] for a in self.axes]
        self.device = lambda stage, by: device(self.axes[stage], by)
        self.sent = []

    def go(self, sem, src, dst, device):
        c = remote(src, dst, self.send.at[sem], self.recv.at[sem], device)
        c.start()
        self.sent.append(c)

    def await_(self, sem, dst):
        remote(dst, dst, self.send.at[sem], self.recv.at[sem], self.device(0, 1)).wait_recv()

    def piece1(self, half, by):
        idx = block("lxyh", self.axes[0], lax.rem(self.at[0] + by, 4))
        return self.part.at[(half,) + idx]

    def start1(self):
        right, left = self.device(0, 1), self.device(0, -1)
        self.go(0, self.piece1(0, 2), self.got1.at[0], right)
        self.go(1, self.piece1(1, 2), self.got1.at[1], left)
        self.go(2, self.piece1(1, 1), self.got1.at[2], right)
        self.go(3, self.piece1(0, 3), self.got1.at[3], left)

    def combine(self):
        for m, by in ((0, 1), (1, 3)):
            self.await_(m, self.got1.at[m])
            mine = self.piece1(m, by)[...]
            self.comb[m] = (self.got1[m].astype(F32) + mine.astype(F32)).astype(BF16)
            self.go(4 + m, self.comb.at[m], self.got1.at[4 + m], self.device(0, 1 if m == 0 else -1))

    def finish1(self):
        for half, raw in ((0, 3), (1, 2)):
            self.await_(raw, self.got1.at[raw])
            self.await_(4 + half, self.got1.at[4 + half])
            total = self.piece1(half, 0)[...].astype(F32)
            total += self.got1[raw].astype(F32) + self.got1[4 + half].astype(F32)
            self.tot1[half] = total.astype(BF16)
        self.direct(1, self.tot1, self.got2, 6)

    def piece(self, stage, ref, by):
        idx = block(self.dims[stage], self.axes[stage], lax.rem(self.at[stage] + by, 4))
        return ref.at[(slice(None),) + idx]

    def direct(self, stage, ref, got, sem):
        for by in (2, 1, 3):
            self.go(sem + by - 1, self.piece(stage, ref, by), got.at[by - 1], self.device(stage, by))

    def summed(self, stage, ref, got, sem):
        total = self.piece(stage, ref, 0)[...].astype(F32)
        for by in (1, 3, 2):
            self.await_(sem + by - 1, got.at[by - 1])
            total += got[by - 1].astype(F32)
        return total

    def finish2(self):
        self.tot2[...] = self.summed(1, self.tot1, self.got2, 6).astype(BF16)
        self.direct(2, self.tot2, self.got3, 9)

    def finish3(self, out):
        total = self.summed(2, self.tot2, self.got3, 9)
        for half in range(2):
            at = self.chunk * 256 + half * 128
            out[:, at : at + 128] = total[half]

    def drain(self):
        for c in self.sent:
            c.wait_send()


def solve_kernel(
    labels_hbm, layout_hbm, lse_hbm, x_hbm, o, q, k, v, do,
    gq_out, gk_out, gv_out, w_out,
    labels, layout, lse, do_v, o_v, x_v, load, gout,
    aux, lab8, labo, xt, xother, ko, vo, qo, doo, auxo, dq_acc, p_s, ds_s,
    dk_b, dv_b, dq_give, dq_got, dq_sum, g, part,
    send, recv, fsend, frecv, xsem, dsend, drecv, osend, orecv, gsend, grecv, rsend, rrecv,
    *bufs,
):
    core, x, y, z_lo, z_hi, dp, ctx = place()
    here = {"x": x, "y": y, "z": z_hi * 2 + z_lo}
    sibling = (dp + 1 - 2 * core, ctx)

    def device(axis, by):
        c = dict(here)
        c[axis] = lax.rem(c[axis] + by + 4, 4)
        return (lax.rem(c["z"], 2) * 8 + c["x"] * 2 + core, c["y"] * 2 + c["z"] // 2)

    ready = greet(
        [target(h) for h in range(4)]
        + [owner(s) for s in range(4)]
        + [sibling]
        + [device(a, by) for a in "xyz" for by in (1, 2, 3)]
    )

    loads = [
        pltpu.make_async_copy(src, dst, load.at[i])
        for i, (src, dst) in enumerate(
            ((labels_hbm, labels), (layout_hbm, layout), (lse_hbm, lse), (do, do_v), (o, o_v), (x_hbm, x_v))
        )
    ]
    for c in loads:
        c.start()
    ready()

    hops = (1, 3, 2, 0)
    arrays = ((k, ko), (v, vo), (q, qo), (do, doo), (aux, auxo), (lab8, labo))
    sends = []

    def give(n, t):
        h = lax.rem(y + t, 4)
        src, dst = arrays[n]
        if n == 5:
            piece = src
        elif n == 4:
            piece = src.at[h]
        else:
            piece = src.at[0, :, pl.ds(pl.multiple_of(h * HD, HD), HD)]
        c = remote(piece, dst.at[y], send.at[n, t], recv.at[n, y], target(h))
        c.start()
        sends.append(c)

    for t in hops:
        give(2, t)
        give(3, t)
    for c in loads[:5]:
        c.wait()
    tiles = tile_rows(labels, layout, ctx)
    labs = jnp.concatenate(
        [jnp.full((1, 128), lab, jnp.int32) for lab, _ in tiles], axis=1
    )
    logs = jnp.concatenate([lg for _, lg in tiles], axis=1)
    for h in range(HEADS):
        cols = slice(h * HD, (h + 1) * HD)
        prod = do_v[0, :, cols].astype(F32) * o_v[0, :, cols].astype(F32)
        delta = jnp.sum(prod.T, axis=0, keepdims=True)
        ln = (logs + lse[0, h : h + 1, :]) * LOG2E
        aux[h, 0:1, :] = ln
        aux[h, 1:2, :] = jnp.where(labs == 1, ln, HIDDEN)
        aux[h, 2:3, :] = jnp.where(labs == 2, ln, HIDDEN)
        aux[h, 3:4, :] = delta
        aux[h, 4:8, :] = jnp.zeros((4, TOK), F32)
    lab8[...] = jnp.broadcast_to(labs.astype(F32), (8, TOK))

    for t in hops:
        give(4, t)
    for t in hops:
        give(5, t)
        give(0, t)
        give(1, t)

    def turn(dst, which):
        def one(i, carry):
            at = pl.multiple_of((2 * i + which) * 256, 256)
            dst[i] = x_v[0, :, pl.ds(at, 256)].T
            return carry

        lax.fori_loop(0, 8, one, 0)

    loads[5].wait()
    turn(xother, 1 - core)
    cross = remote(xother, xt.at[1], xsem.at[0], xsem.at[1], sibling)
    cross.start()
    turn(xt.at[0], core)
    dq_acc[...] = jnp.zeros_like(dq_acc)

    def arrived(ref, sem):
        remote(ref, ref, send.at[0, 0], sem, sibling).wait_recv()

    def left(ref, sem):
        remote(ref, ref, sem, recv.at[0, 0], sibling).wait_send()

    def slot(i):
        return lax.rem(y + jnp.where(i == 0, 3, jnp.where(i == 3, 0, i)), 4)

    near = (3, 1, 2, 0)
    for t in near:
        s = lax.rem(y + t, 4)
        for n in (2, 3, 4):
            dst = arrays[n][1]
            arrived(dst.at[s], recv.at[n, s])
            remote(dst.at[s], dst.at[4 + s], fsend.at[n - 2, s], frecv.at[n - 2, s], sibling).start()
    for t in near:
        s = lax.rem(y + t, 4)
        for n in (2, 3, 4):
            arrived(arrays[n][1].at[4 + s], frecv.at[n - 2, s])

    def keys(i, carry):
        s = slot(i)
        for n in (5, 0, 1):
            arrived(arrays[n][1].at[s], recv.at[n, s])
        k_b = ko[s]
        v_b = vo[s]
        for c in range(4):
            pair = slice(2 * c, 2 * c + 2)
            sc = dot_t(k_b, qo[pair].reshape(2 * TOK, HD))
            dp_ = dot_t(v_b, doo[pair].reshape(2 * TOK, HD))
            rows = jnp.concatenate([auxo[2 * c], auxo[2 * c + 1]], axis=1)
            delta = rows[3:4, :]
            cols = slice(c * 2 * TOK, (c + 1) * 2 * TOK)
            for t in range(2):
                part_ = slice(t * 128, (t + 1) * 128)
                lab = labo[s, 0:1, t * 128 : t * 128 + 1]
                row = jnp.where(
                    lab == 0.0, rows[0:1, :], jnp.where(lab == 1.0, rows[1:2, :], rows[2:3, :])
                )
                p = jnp.exp2(sc[part_] * (SCALE * LOG2E) - row)
                p_s[part_, cols] = p.astype(BF16)
                ds_s[part_, cols] = (p * (dp_[part_] - delta) * SCALE).astype(BF16)
        q_all = qo[...].reshape(8 * TOK, HD)
        do_all = doo[...].reshape(8 * TOK, HD)
        dv_b[s] = dot_n(p_s[...], do_all).astype(BF16)
        remote(dv_b.at[s], g.at[0, 2, y], osend.at[2, s], orecv.at[2, y], owner(s)).start()
        dk_b[s] = dot_n(ds_s[...], q_all).astype(BF16)
        remote(dk_b.at[s], g.at[0, 1, y], osend.at[1, s], orecv.at[1, y], owner(s)).start()
        dq_acc[...] += dot_l(ds_s[...], k_b).reshape(8, TOK, HD)
        return carry

    lax.fori_loop(0, 4, keys, 0)
    for t in (2, 3, 1, 0):
        s = lax.rem(y + t, 4)
        dq_give[s] = dq_acc[4 + s].astype(BF16)
        remote(dq_give.at[s], dq_got.at[s], dsend.at[s], drecv.at[s], sibling).start()
    for t in (2, 3, 1, 0):
        s = lax.rem(y + t, 4)
        arrived(dq_got.at[s], drecv.at[s])
        dq_sum[s] = (dq_acc[s] + dq_got[s].astype(F32)).astype(BF16)
        remote(dq_sum.at[s], g.at[0, 0, y], osend.at[0, s], orecv.at[0, y], owner(s)).start()

    def relay(*parts):
        for t, n in ((t, n) for t in (1, 3, 2, 0) for n in parts):
            h = lax.rem(y + t, 4)
            arrived(g.at[0, n, h], orecv.at[n, h])
            remote(g.at[0, n, h], g.at[1, n, h], gsend.at[n, h], grecv.at[n, h], sibling).start()

    def whole(n):
        for h in range(4):
            arrived(g.at[1, n, h], grecv.at[n, h])

    jobs = []
    for c, (n, j) in enumerate(CHUNKS):
        jobs.append(
            Job(
                n, j, ORDERS[c % 3], part, bufs[6 * c : 6 * c + 6],
                (rsend.at[c], rrecv.at[c]), here, device,
            )
        )

    def gemm(n, j):
        rhs = jnp.concatenate(
            [jnp.concatenate([g[c, n, 2 * j], g[c, n, 2 * j + 1]], axis=1) for c in range(2)], axis=0
        )

        def rows(i, carry):
            lhs = jnp.concatenate(
                [xt[c, pl.ds(i * 4, 4)].reshape(1024, TOK) for c in range(2)], axis=1
            )
            res = dot_n(lhs, rhs).astype(BF16)
            for half in range(2):
                part[2 * n + j, half, i] = res[:, half * 128 : (half + 1) * 128].reshape(
                    4, 4, 2, 32, 128
                )
            return carry

        lax.fori_loop(0, 2, rows, 0)

    cross.wait()
    first, second = jobs[:3], jobs[3:]
    relay(2, 1)
    whole(2)
    for c in range(2):
        gemm(*CHUNKS[c])
        first[c].start1()
    whole(1)
    gemm(*CHUNKS[2])
    first[2].start1()
    gemm(*CHUNKS[3])
    relay(0)
    whole(0)
    gemm(*CHUNKS[4])
    gemm(*CHUNKS[5])
    for one, two in zip(first, second):
        one.combine()
        two.start1()
    outs = [
        pltpu.make_async_copy(g.at[0, n, h], dst.at[0, :, h * HD : (h + 1) * HD], gout.at[n, h])
        for n, dst in enumerate((gq_out, gk_out, gv_out))
        for h in range(HEADS)
    ]
    for c in outs:
        c.start()
    for one, two in zip(first, second):
        one.finish1()
        two.combine()
    for one in first:
        one.finish2()
    for two in second:
        two.finish1()
    for one in first:
        one.finish3(w_out)
    for two in second:
        two.finish2()
    for two in second:
        two.finish3(w_out)

    for job in jobs:
        job.drain()
    for c in outs:
        c.wait()
    for c in sends:
        c.wait_send()
    for s in range(4):
        for n in (2, 3, 4):
            left(arrays[n][1].at[s], fsend.at[n - 2, s])
        left(dq_give.at[s], dsend.at[s])
        for n in range(3):
            left(dq_sum.at[s], osend.at[n, s])
            left(g.at[0, n, s], gsend.at[n, s])


def solve(labels, layout, lse, q, k, v, o, do, x_in):
    blk = lambda *n: pltpu.VMEM((*n, TOK, HD), BF16)
    sem = lambda *n: pltpu.SemaphoreType.DMA(n)
    scratch = [
        pltpu.SMEM((1, 16), jnp.int32),
        pltpu.SMEM((1, 16), jnp.int32),
        pltpu.VMEM((1, 4, TOK), F32),
        pltpu.VMEM((1, TOK, 512), BF16),
        pltpu.VMEM((1, TOK, 512), BF16),
        pltpu.VMEM((1, TOK, 4096), BF16),
        sem(6),
        sem(3, 4),
        pltpu.VMEM((4, 8, TOK), F32),
        pltpu.VMEM((8, TOK), F32),
        pltpu.VMEM((4, 8, TOK), F32),
        pltpu.VMEM((2, 8, 256, TOK), BF16),
        pltpu.VMEM((8, 256, TOK), BF16),
        blk(4), blk(4), blk(8), blk(8),
        pltpu.VMEM((8, 8, TOK), F32),
        pltpu.VMEM((8, TOK, HD), F32),
        pltpu.VMEM((TOK, 2048), BF16),
        pltpu.VMEM((TOK, 2048), BF16),
        blk(4), blk(4),
        blk(4), blk(4), blk(4),
        blk(2, 3, 4),
        pltpu.VMEM((6, 2, 2, 4, 4, 2, 32, 128), BF16),
        sem(6, 4), sem(6, 4), sem(3, 4), sem(3, 4), sem(2), sem(4), sem(4),
        sem(3, 4), sem(3, 4), sem(3, 4), sem(3, 4), sem(6, 12), sem(6, 12),
    ]
    for c in range(6):
        dims = ["lxyh"]
        for axis in ORDERS[c % 3]:
            dims.append(left_over(dims[-1], axis))
        s1, s2, s3 = [tuple(SIZES[d] for d in ds) + (32, 128) for ds in dims[1:]]
        for shape in ((6,) + s1, (2,) + s1, (2,) + s1, (3, 2) + s2, (2,) + s2, (3, 2) + s3):
            scratch.append(pltpu.VMEM(shape, BF16))
    return pl.pallas_call(
        solve_kernel,
        out_shape=(
            *(jax.ShapeDtypeStruct((1, TOK, HEADS * HD), BF16),) * 3,
            jax.ShapeDtypeStruct((32, 1536), F32),
        ),
        in_specs=[ANY] * 9,
        out_specs=(ANY, ANY, ANY, VM),
        scratch_shapes=scratch,
        compiler_params=pltpu.CompilerParams(collective_id=0, has_side_effects=True),
        name="solve",
    )(labels, layout, lse, x_in, o, q, k, v, do)


def finish_kernel(*refs):
    ins, outs, bufs = refs[:4], refs[4:8], refs[8:12]
    got, put = refs[12:]
    loads = [pltpu.make_async_copy(a, b, got.at[i]) for i, (a, b) in enumerate(zip(ins, bufs))]
    stores = [pltpu.make_async_copy(a, b, put.at[i]) for i, (a, b) in enumerate(zip(bufs, outs))]
    for c in loads:
        c.start()
    for a, b in zip(loads, stores):
        a.wait()
        b.start()
    for c in stores:
        c.wait()


def finish(*arrays):
    return pl.pallas_call(
        finish_kernel,
        out_shape=tuple(jax.ShapeDtypeStruct(a.shape, a.dtype) for a in arrays),
        in_specs=[ANY] * 4,
        out_specs=(ANY,) * 4,
        scratch_shapes=[pltpu.VMEM(a.shape, a.dtype) for a in arrays]
        + [pltpu.SemaphoreType.DMA((4,))] * 2,
        name="finish",
    )(*arrays)


def per_device(inputs, queries, keys, values, attn_out, grad_out, lse_shift, labels, layout):
    grads = solve(labels, layout, lse_shift, queries, keys, values, attn_out, grad_out, inputs)
    return finish(*grads)


def solution(mesh):
    tok = P("dp", "ctx", None)
    return jax.shard_map(
        per_device,
        mesh=mesh,
        in_specs=(tok,) * 6 + (P("dp", None, "ctx"), P("dp", None), P("dp", None)),
        out_specs=(tok, tok, tok, P(("dp", "ctx"), None)),
        check_vma=False,
    )
```
